32 devices in a mesh: tm: 8 (over z, x), rows: 4 (over y, core).
Axes of the slice: x: 2, y: 2, z: 4, core: 2. Of those that a mesh axis runs over, the one named last changes fastest.
Arguments:
- clip: float32 [32, 8, 32, 128], P('tm', 'rows'), may hold values from -6 to 6
- kernel_one: float32 [3, 3, 3, 128, 128], replicated, may hold values from -0.109375 to 0.109375
- kernel_two: float32 [3, 3, 3, 128, 128], replicated, may hold values from -0.109375 to 0.109375
- cotangent: float32 [32, 8, 32, 128], P('tm', 'rows'), may hold values from -6 to 6
Outputs:
- block_out: float32 [32, 8, 32, 128], P('tm', 'rows')
- grad_clip: float32 [32, 8, 32, 128], P('tm', 'rows')
- grad_one: float32 [3, 3, 3, 128, 128], replicated
- grad_two: float32 [3, 3, 3, 128, 128], replicated
The draws below stay inside these ranges and needn't reach their ends.
All inputs are finite; a program needn't handle non-finite values.
Results may differ from the reference program's by a relative error of at most 0.00014.
Values sent between devices are 32-bit elements; how exact they have to be, the bound alone decides.
No kernel may reach another device: no remote copies, remote signals or barrier semaphores. Data moves between devices by JAX's collectives and lax.ppermute only.
A program may use at most 128 MiB of HBM per device.

```python
import math
import jax
import jax.numpy as jnp
from jax import lax

CH = 128
WIDTH = 32
FRAMES = 32
HEIGHT = 8


def block_levels(own_key, dims, shards, smallest, largest):
    loudness, own = 1.0, jax.random.fold_in(own_key, 6)
    for dim, blocks in shards:
        draws = jnp.exp(jax.random.uniform(jax.random.fold_in(own, dim), (blocks,), jnp.float32, smallest / len(shards), largest / len(shards)))
        loudness = loudness * jnp.repeat(draws, dims[dim] // blocks).reshape([-1 if axis == dim else 1 for axis in range(len(dims))])
    return loudness


def scatter_about(rng, dims, spread, limit, cuts=(), held_as=jnp.bfloat16):
    loudness = block_levels(rng, dims, cuts, -0.22, 0.18) if cuts else 1.0
    values = jax.random.normal(rng, dims, jnp.float32) * spread * loudness
    return jnp.minimum(jnp.maximum(values, -limit), limit).astype(held_as)


def setup_inputs(seed: int = 0) -> dict:
    streams_of = jax.random.split(jax.random.key(seed), 5)
    clip = scatter_about(streams_of[0], (FRAMES, HEIGHT, WIDTH, CH), 1.0, 6.0, ((0, 8), (1, 4)), jnp.float32)
    kernel_one = scatter_about(streams_of[1], (3, 3, 3, CH, CH), (27 * CH) ** -0.5, 0.109375, (), jnp.float32)
    kernel_two = scatter_about(streams_of[2], (3, 3, 3, CH, CH), (27 * CH) ** -0.5, 0.109375, (), jnp.float32)
    cotangent = scatter_about(streams_of[3], (FRAMES, HEIGHT, WIDTH, CH), 1.0, 6.0, ((0, 8), (1, 4)), jnp.float32)
    return {"clip": clip, "kernel_one": kernel_one, "kernel_two": kernel_two, "cotangent": cotangent}


def convolve(field, kernel):
    result = lax.conv_general_dilated(field[None], kernel, (1, 1, 1), ((2, 0), (1, 1), (1, 1)), dimension_numbers=('NDHWC', 'DHWIO', 'NDHWC'), precision=lax.Precision.HIGHEST)
    return result[0]

def forward(clip, kernel_one, kernel_two):
    return clip + convolve(jax.nn.silu(convolve(clip, kernel_one)), kernel_two)

def reference(clip, kernel_one, kernel_two, cotangent):
    block_out, pullback = jax.vjp(forward, clip, kernel_one, kernel_two)
    grad_clip, grad_one, grad_two = pullback(cotangent)
    factor = 1.0 / math.sqrt(FRAMES * HEIGHT * WIDTH)
    return (block_out, grad_clip, grad_one * factor, grad_two * factor)
```

```python
import math

import jax
import jax.numpy as jnp
from jax import lax
from jax.experimental import pallas as pl
from jax.experimental.pallas import tpu as pltpu
from jax.sharding import PartitionSpec as P

F32, BF16 = jnp.float32, jnp.bfloat16
VM = pltpu.VMEM


def shaped(*dims, kind=F32):
    return jax.ShapeDtypeStruct(dims, kind)


def kernel(body, outs, args, scratch=(), flops=0, name=None, limit=20):
    moved = sum(a.size * a.dtype.itemsize for a in (*args, *outs))
    return pl.pallas_call(
        body,
        out_shape=list(outs),
        in_specs=[pl.BlockSpec(memory_space=VM)] * len(args),
        out_specs=[pl.BlockSpec(memory_space=VM)] * len(outs),
        scratch_shapes=list(scratch),
        compiler_params=pltpu.CompilerParams(vmem_limit_bytes=limit << 20),
        cost_estimate=pl.CostEstimate(flops=flops, bytes_accessed=moved, transcendentals=0),
        name=name,
    )(*args)


def halves(value):
    high = value.astype(BF16)
    return high, (value - high.astype(F32)).astype(BF16)


def moved_column(value, step, span):
    if step == 0:
        return value
    count = value.shape[0]
    column = lax.broadcasted_iota(jnp.int32, value.shape, 0) % span
    edge = span - 1 if step > 0 else 0
    return jnp.where(column == edge, 0.0, pltpu.roll(value, (-step) % count, 0))


def weights_body(plain, turned, plain_out, turned_out):
    taps, ch = plain.shape[0], plain.shape[1]

    def step(tap, carry):
        high, low = halves(plain[tap])
        plain_out[tap, :, 0:ch] = high
        plain_out[tap, :, ch : 2 * ch] = low
        high, low = halves(turned[taps - 1 - tap].T)
        turned_out[tap, :, 0:ch] = high
        turned_out[tap, :, ch : 2 * ch] = low
        return carry

    lax.fori_loop(0, taps, step, 0)


def weights(plain, turned, name):
    taps, ch = plain.shape[0], plain.shape[1]
    out = shaped(taps, ch, 2 * ch, kind=BF16)
    return kernel(weights_body, [out, out], (plain, turned), name=name)


def pack_body(first, second, before, after, whole, outer, inner):
    frames = first.shape[0]
    depth = whole.shape[1] - frames
    lead = before.shape[0] - depth
    rows = first.shape[1]
    odd = lax.axis_index("rows") % 2
    whole[0, depth:] = first[...]
    whole[0, 0:depth] = before[lead:]
    whole[1, 0:frames] = second[...]
    whole[1, frames:] = after[0:depth]
    outer[...] = whole[:, :, odd * (rows - 1)]
    inner[...] = whole[:, :, (1 - odd) * (rows - 1)]


def pack(first, second, before, after, name):
    frames, rows, span, ch = first.shape
    edge = shaped(2, frames + 2, span, ch)
    return kernel(
        pack_body,
        [shaped(2, frames + 2, rows, span, ch), edge, edge],
        (first, second, before, after),
        name=name,
    )


def convolve(strip, weight, shifted, columns):
    tall, wide, span, ch = strip.shape
    frames, rows = tall - 2, wide - 2
    cells = frames * rows * span
    flat = strip[...].reshape(tall * wide * span, ch)
    for c in range(3):
        high, low = halves(moved_column(flat, c - 1, span))
        shifted[0, c] = high.reshape(tall, wide, span, ch)
        shifted[1, c] = low.reshape(tall, wide, span, ch)
    for part in range(2):
        for a in range(3):
            for b in range(3):
                for c in range(3):
                    tap = (a * 3 + b) * 3 + c
                    piece = shifted[part, c, a : a + frames, b : b + rows]
                    columns[part, :, tap * ch : (tap + 1) * ch] = piece.reshape(cells, ch)
    matrix = weight[...].reshape(27 * ch, 2 * ch)
    main = jnp.dot(columns[0], matrix, preferred_element_type=F32)
    rest = jnp.dot(columns[1], matrix[:, :ch], preferred_element_type=F32)
    return main[:, :ch] + main[:, ch:] + rest


def conv_scratch(frames, rows, span, ch):
    return [
        pltpu.VMEM((frames + 2, rows + 2, span, ch), F32),
        pltpu.VMEM((2, 3, frames + 2, rows + 2, span, ch), BF16),
        pltpu.VMEM((2, frames * rows * span, 27 * ch), BF16),
    ]


def place_rows(strip, own, outer, inner, odd):
    rows = own.shape[1]
    strip[:, 1 : rows + 1] = own
    strip[:, odd * (rows + 1)] = outer
    strip[:, (1 - odd) * (rows + 1)] = inner


def forward_body(own, partner, outer, w_one, w_two, active, delta, tail, head, crossing, strip, shifted, columns):
    odd = lax.axis_index("rows") % 2
    rows = own.shape[2]
    near = odd * (rows - 1)
    place_rows(strip, own[0], outer[0], partner[0, :, near], odd)
    pre = convolve(strip, w_one, shifted, columns)
    place_rows(strip, own[1], outer[1], partner[1, :, near], odd)
    slope = convolve(strip, w_two, shifted, columns)
    gate = jax.nn.sigmoid(pre)
    act = (pre * gate).reshape(active.shape)
    dlt = (slope * gate * (1.0 + pre * (1.0 - gate))).reshape(delta.shape)
    active[...] = act
    delta[...] = dlt
    tail[...] = act[active.shape[0] - 2 :]
    head[...] = dlt[:2]
    crossing[...] = jnp.where(odd == 0, dlt, act)


def outputs_body(ext, outer, inner, w_two, w_one, clip, cotangent, block_out, grad_clip, strip, shifted, columns):
    odd = lax.axis_index("rows") % 2
    place_rows(strip, ext[0], outer[0], inner[0], odd)
    block_out[...] = clip[...] + convolve(strip, w_two, shifted, columns).reshape(clip.shape)
    place_rows(strip, ext[1], outer[1], inner[1], odd)
    grad_clip[...] = cotangent[...] + convolve(strip, w_one, shifted, columns).reshape(clip.shape)


def grads_body(sending, own, partner, outer, far, active, delta, arrived, first, second, field, wide, turned):
    odd = lax.axis_index("rows") % 2
    y_bit = (lax.axis_index("rows") // 2) % 2
    x_bit = lax.axis_index("tm") % 2
    tall, rows, span, ch = own.shape[1:]
    frames = active.shape[0]
    pick = 1 - odd
    field[:, pl.ds(1 + rows * odd, rows)] = own[pick]
    field[:, pl.ds(1 + rows * (1 - odd), rows)] = partner[pick]
    field[:, odd * (2 * rows + 1)] = outer[pick]
    field[:, (1 - odd) * (2 * rows + 1)] = far[pick]
    flat = field[...].reshape(tall * (2 * rows + 2) * span, ch)
    for c in range(3):
        high, low = halves(moved_column(flat, c - 1, span))
        wide[c, :, :, :, 0:ch] = high.reshape(field.shape)
        wide[c, :, :, :, ch : 2 * ch] = low.reshape(field.shape)
    mine = jnp.where(odd == 0, active[...], delta[...])
    other = arrived[...]
    swap = odd == 1
    upper = jnp.where(swap, other, mine)
    lower = jnp.where(swap, mine, other)
    cells = frames * 2 * rows * span
    joined = jnp.concatenate([upper, lower], 1).reshape(cells, ch).T
    high, low = halves(joined)
    turned[0:ch] = high
    turned[ch : 2 * ch] = low

    def tap_of(group, j):
        tap = jnp.minimum(group * 7 + j, 26)
        a, b, c = tap // 9, (tap // 3) % 3, tap % 3
        piece = wide[c, pl.ds(a, frames), pl.ds(b, 2 * rows)].reshape(cells, 2 * ch)
        product = jnp.dot(turned[...], piece, preferred_element_type=F32)
        left = product[:, :ch] + product[:, ch:]
        return left[:ch] + left[ch:]

    def step(j, carry):
        first[j] = tap_of(y_bit ^ sending, j)
        second[j] = tap_of(2 + (x_bit ^ sending), j)
        return carry

    lax.fori_loop(0, 7, step, 0, unroll=True)


def grads(sending, own, partner, outer, far, active, delta, arrived, name):
    frames, rows, span, ch = active.shape
    out = shaped(7, ch, ch)
    field = (frames + 2, 2 * rows + 2, span, ch)
    return kernel(
        lambda *refs: grads_body(sending, *refs),
        [out, out],
        (own, partner, outer, far, active, delta, arrived),
        scratch=[
            pltpu.VMEM(field, F32),
            pltpu.VMEM((3, *field[:-1], 2 * ch), BF16),
            pltpu.VMEM((2 * ch, frames * 2 * rows * span), BF16),
        ],
        flops=14 * 2 * (2 * ch) ** 2 * frames * 2 * rows * span,
        name=name,
    )


def halve_body(keep_a, keep_b, got_a, got_b, stay_a, go_a, stay_b, go_b):
    x_bit = lax.axis_index("tm") % 2
    y_bit = (lax.axis_index("rows") // 2) % 2
    half = stay_a.shape[0]
    for keep, got, bit, stay, go in ((keep_a, got_a, x_bit, stay_a, go_a), (keep_b, got_b, y_bit, stay_b, go_b)):
        near = pl.ds(pl.multiple_of(bit * half, 8), half)
        away = pl.ds(pl.multiple_of((1 - bit) * half, 8), half)
        go[...] = keep[away] + got[away]
        stay[...] = keep[near] + got[near]


def quarter_body(keep_a, keep_b, got_a, got_b, *outs):
    z = (lax.axis_index("tm") // 2) % 4
    size = outs[0].shape[1]
    for d in range(4):
        part = pl.ds(pl.multiple_of((z ^ d) * size, 8), size)
        outs[d][0] = keep_a[part] + got_a[part]
        outs[d][1] = keep_b[part] + got_b[part]


def total_body(factor, *refs):
    *parts, out = refs
    value = parts[0][...]
    for part in parts[1:]:
        value = value + part[...]
    out[...] = value * factor


def join_quarters_body(q0, q1, q2, q3, out_a, out_b):
    z = (lax.axis_index("tm") // 2) % 4
    size = q0.shape[1]
    for d, quarter in enumerate((q0, q1, q2, q3)):
        part = pl.ds(pl.multiple_of((z ^ d) * size, 8), size)
        out_a[part] = quarter[0]
        out_b[part] = quarter[1]


def join_halves_body(own_a, got_a, own_b, got_b, out_a, out_b):
    x_bit = lax.axis_index("tm") % 2
    y_bit = (lax.axis_index("rows") // 2) % 2
    half = own_a.shape[0]
    for own, got, bit, out in ((own_a, got_a, x_bit, out_a), (own_b, got_b, y_bit, out_b)):
        out[pl.ds(pl.multiple_of(bit * half, 8), half)] = own[...]
        out[pl.ds(pl.multiple_of((1 - bit) * half, 8), half)] = got[...]


def finish_body(a0, a1, b0, b1, ca0, ca1, cb0, cb1, one, two):
    odd = lax.axis_index("rows") % 2
    x_bit = lax.axis_index("tm") % 2
    y_bit = (lax.axis_index("rows") // 2) % 2
    groups = ((a0, ca0, y_bit), (a1, ca1, 1 - y_bit), (b0, cb0, 2 + x_bit), (b1, cb1, 3 - x_bit))

    for mine, other, group in groups:

        def step(j, carry, mine=mine, other=other, group=group):
            tap = group * 7 + j

            @pl.when(tap < 27)
            def _():
                left, right = mine[j], other[j]
                two[26 - tap] = jnp.where(odd == 0, left, right)
                one[tap] = jnp.where(odd == 0, right, left).T

            return carry

        lax.fori_loop(0, 7, step, 0)


def swapped(value, axis, bits):
    count = lax.axis_size(axis)
    return lax.ppermute(value, axis, [(i, i ^ bits) for i in range(count)])


def per_device(clip, kernel_one, kernel_two, cotangent):
    frames, rows, span, ch = clip.shape
    tm, strips = lax.axis_size("tm"), lax.axis_size("rows")
    factor = 1.0 / math.sqrt(frames * tm * rows * strips * span)
    later = [(i, i + 1) for i in range(tm - 1)]
    earlier = [(i + 1, i) for i in range(tm - 1)]
    across = [pair for i in range(1, strips - 1, 2) for pair in ((i, i + 1), (i + 1, i))]

    before = lax.ppermute(clip, "tm", later)
    after = lax.ppermute(cotangent, "tm", earlier)
    one, two = kernel_one.reshape(27, ch, ch), kernel_two.reshape(27, ch, ch)
    one_plain, two_turned = weights(one, two, "weights_early")
    own, edge, _ = pack(clip, cotangent, before, after, "pack_inputs")
    outer = lax.ppermute(edge, "rows", across)
    partner = swapped(own, "rows", 1)
    far = swapped(outer, "rows", 1)

    cell = shaped(frames, rows, span, ch)
    strip = shaped(2, rows, span, ch)
    conv_flops = 3 * 2 * frames * rows * span * 27 * ch * ch
    active, delta, tail, head, crossing = kernel(
        forward_body,
        [cell, cell, strip, strip, cell],
        (own, partner, outer, one_plain, two_turned),
        scratch=conv_scratch(frames, rows, span, ch),
        flops=2 * conv_flops,
        name="forward",
    )
    arrived = swapped(crossing, "rows", 1)

    shared = (own, partner, outer, far, active, delta, arrived)
    give_a, give_b = grads(1, *shared, "grads_give")
    got_a = swapped(give_a, "rows", 2)
    got_b = swapped(give_b, "tm", 1)
    keep_a, keep_b = grads(0, *shared, "grads_keep")

    size = 7 * ch
    half = shaped(size // 2, ch)
    stay_a, go_a, stay_b, go_b = kernel(
        halve_body,
        [half] * 4,
        tuple(v.reshape(size, ch) for v in (keep_a, keep_b, got_a, got_b)),
        name="halve",
    )
    got_a = swapped(go_a, "tm", 1)
    got_b = swapped(go_b, "rows", 2)
    quarter = shaped(2, size // 8, ch)
    parts = kernel(quarter_body, [quarter] * 4, (stay_a, stay_b, got_a, got_b), name="quarter")
    summed = [parts[0]] + [swapped(parts[d], "tm", 2 * d) for d in range(1, 4)]
    wider = [("tm", 1 << k) for k in range(3, tm.bit_length() - 1)]
    wider += [("rows", 1 << k) for k in range(2, strips.bit_length() - 1)]
    for axis, bits in wider:
        (shard,) = kernel(lambda *refs: total_body(1.0, *refs), [quarter], summed, name="total")
        summed = [shard, swapped(shard, axis, bits)]
    (shard,) = kernel(lambda *refs: total_body(factor, *refs), [quarter], summed, name="total")

    quarters = [shard] + [swapped(shard, "tm", 2 * d) for d in range(1, 4)]
    own_a, own_b = kernel(join_quarters_body, [half] * 2, quarters, name="join_quarters")
    got_a = swapped(own_a, "tm", 1)
    got_b = swapped(own_b, "rows", 2)
    full = shaped(size, ch)
    all_a, all_b = kernel(join_halves_body, [full] * 2, (own_a, got_a, own_b, got_b), name="join_halves")
    got_a = swapped(all_a, "rows", 2)
    got_b = swapped(all_b, "tm", 1)
    mine = [all_a, got_a, all_b, got_b]
    others = [swapped(v, "rows", 1) for v in mine]
    grad = shaped(27, ch, ch)
    grad_one, grad_two = kernel(
        finish_body,
        [grad, grad],
        [v.reshape(7, ch, ch) for v in mine + others],
        name="finish",
    )

    two_plain, one_turned = weights(two, one, "weights_late")
    before = lax.ppermute(tail, "tm", later)
    after = lax.ppermute(head, "tm", earlier)
    ext, edge, inside = pack(active, delta, before, after, "pack_middle")
    outer = lax.ppermute(edge, "rows", across)
    inner = swapped(inside, "rows", 1)
    block_out, grad_clip = kernel(
        outputs_body,
        [cell, cell],
        (ext, outer, inner, two_plain, one_turned, clip, cotangent),
        scratch=conv_scratch(frames, rows, span, ch),
        flops=2 * conv_flops,
        name="outputs",
    )
    shape = kernel_one.shape
    return block_out, grad_clip, grad_one.reshape(shape), grad_two.reshape(shape)


def solution(mesh):
    return jax.shard_map(
        per_device,
        mesh=mesh,
        in_specs=(P("tm", "rows", None, None), P(), P(), P("tm", "rows", None, None)),
        out_specs=(P("tm", "rows", None, None), P("tm", "rows", None, None), P(), P()),
        check_vma=False,
    )
```

```python
import math

import jax
import jax.numpy as jnp
from jax import lax
from jax.experimental import pallas as pl
from jax.experimental.pallas import tpu as pltpu
from jax.sharding import PartitionSpec as P

F32, BF16 = jnp.float32, jnp.bfloat16
VM, HBM = pltpu.VMEM, pltpu.HBM


def shaped(*dims, kind=F32):
    return jax.ShapeDtypeStruct(dims, kind)


def kernel(body, outs, args, scratch=(), flops=0, name=None, limit=20, far_in=(), far_out=(), alias=None):
    moved = sum(a.size * a.dtype.itemsize for a in (*args, *outs))
    args = [pltpu.with_memory_space_constraint(a, HBM) if i in far_in else a for i, a in enumerate(args)]
    return pl.pallas_call(
        body,
        out_shape=list(outs),
        in_specs=[pl.BlockSpec(memory_space=HBM if i in far_in else VM) for i in range(len(args))],
        out_specs=[pl.BlockSpec(memory_space=HBM if i in far_out else VM) for i in range(len(outs))],
        scratch_shapes=list(scratch),
        input_output_aliases=alias or {},
        compiler_params=pltpu.CompilerParams(vmem_limit_bytes=limit << 20),
        cost_estimate=pl.CostEstimate(flops=flops, bytes_accessed=moved, transcendentals=0),
        name=name,
    )(*args)


def halves(value):
    high = value.astype(BF16)
    return high, (value - high.astype(F32)).astype(BF16)


def moved_column(value, step, span):
    if step == 0:
        return value
    count = value.shape[0]
    column = lax.broadcasted_iota(jnp.int32, value.shape, 0) % span
    edge = span - 1 if step > 0 else 0
    return jnp.where(column == edge, 0.0, pltpu.roll(value, (-step) % count, 0))


def weights_body(plain, turned, *refs):
    count = (len(refs) - 4) // 2
    extra, (plain_out, turned_out), near = refs[:count], refs[count : count + 2], refs[count + 2 : -2]
    held, sem = refs[-2:]
    taps, ch = plain.shape[0], plain.shape[1]
    block = taps // 3
    copies = []
    for k in range(3):
        part = pl.ds(k * block, block)
        for which, source in enumerate((plain, turned)):
            copies.append(pltpu.make_async_copy(source.at[part], held.at[which, part], sem.at[which, k]))
    side = [pltpu.make_async_copy(a, b, sem.at[2, k]) for k, (a, b) in enumerate(zip(extra, near))]
    for copy in (*copies, *side):
        copy.start()

    def step(tap, carry):
        high, low = halves(held[0, tap])
        plain_out[tap, :, 0:ch] = high
        plain_out[tap, :, ch : 2 * ch] = low
        high, low = halves(held[1, tap].T)
        turned_out[taps - 1 - tap, :, 0:ch] = high
        turned_out[taps - 1 - tap, :, ch : 2 * ch] = low
        return carry

    for k in range(3):
        copies[2 * k].wait()
        copies[2 * k + 1].wait()
        lax.fori_loop(k * block, (k + 1) * block, step, 0)
    for copy in side:
        copy.wait()


def weights(plain, turned, extra, name):
    taps, ch = plain.shape[0], plain.shape[1]
    out = shaped(taps, ch, 2 * ch, kind=BF16)
    return kernel(
        weights_body,
        [out, out, *(shaped(*v.shape) for v in extra)],
        (plain, turned, *extra),
        scratch=[pltpu.VMEM((2, taps, ch, ch), F32), pltpu.SemaphoreType.DMA((3, 3))],
        far_in=range(2 + len(extra)),
        name=name,
    )


def ends_body(first, second, tail, head, sem):
    frames, depth = first.shape[0], tail.shape[0]
    one = pltpu.make_async_copy(first.at[pl.ds(frames - depth, depth)], tail, sem.at[0])
    two = pltpu.make_async_copy(second.at[pl.ds(0, depth)], head, sem.at[1])
    one.start()
    two.start()
    one.wait()
    two.wait()


def pack_body(first, second, before, after, whole, outer, inner):
    frames = first.shape[0]
    depth = whole.shape[1] - frames
    lead = before.shape[0] - depth
    rows = first.shape[1]
    odd = lax.axis_index("rows") % 2
    whole[0, depth:] = first[...]
    whole[0, 0:depth] = before[lead:]
    whole[1, 0:frames] = second[...]
    whole[1, frames:] = after[0:depth]
    outer[...] = whole[:, :, odd * (rows - 1)]
    inner[...] = whole[:, :, (1 - odd) * (rows - 1)]


def pack(first, second, before, after, name):
    frames, rows, span, ch = first.shape
    edge = shaped(2, frames + 2, span, ch)
    return kernel(
        pack_body,
        [shaped(2, frames + 2, rows, span, ch), edge, edge],
        (first, second, before, after),
        name=name,
    )


def convolve(strip, weight, shifted, columns):
    tall, wide, span, ch = strip.shape
    frames, rows = tall - 2, wide - 2
    cells = frames * rows * span
    flat = strip[...].reshape(tall * wide * span, ch)
    for c in range(3):
        high, low = halves(moved_column(flat, c - 1, span))
        shifted[0, c] = high.reshape(tall, wide, span, ch)
        shifted[1, c] = low.reshape(tall, wide, span, ch)
    for part in range(2):
        for a in range(3):
            for b in range(3):
                for c in range(3):
                    tap = (a * 3 + b) * 3 + c
                    piece = shifted[part, c, a : a + frames, b : b + rows]
                    columns[part, :, tap * ch : (tap + 1) * ch] = piece.reshape(cells, ch)
    matrix = weight[...].reshape(27 * ch, 2 * ch)
    main = jnp.dot(columns[0], matrix, preferred_element_type=F32)
    rest = jnp.dot(columns[1], matrix[:, :ch], preferred_element_type=F32)
    return main[:, :ch] + main[:, ch:] + rest


def conv_scratch(frames, rows, span, ch):
    return [
        pltpu.VMEM((frames + 2, rows + 2, span, ch), F32),
        pltpu.VMEM((2, 3, frames + 2, rows + 2, span, ch), BF16),
        pltpu.VMEM((2, frames * rows * span, 27 * ch), BF16),
    ]


def place_rows(strip, own, outer, inner, odd):
    rows = own.shape[1]
    strip[:, 1 : rows + 1] = own
    strip[:, odd * (rows + 1)] = outer
    strip[:, (1 - odd) * (rows + 1)] = inner


def forward_body(own, partner, outer, w_one, w_two, active, delta, tail, head, crossing, strip, shifted, columns):
    odd = lax.axis_index("rows") % 2
    rows = own.shape[2]
    near = odd * (rows - 1)
    place_rows(strip, own[0], outer[0], partner[0, :, near], odd)
    pre = convolve(strip, w_one, shifted, columns)
    place_rows(strip, own[1], outer[1], partner[1, :, near], odd)
    slope = convolve(strip, w_two, shifted, columns)
    gate = jax.nn.sigmoid(pre)
    act = (pre * gate).reshape(active.shape)
    dlt = (slope * gate * (1.0 + pre * (1.0 - gate))).reshape(delta.shape)
    active[...] = act
    delta[...] = dlt
    tail[...] = act[active.shape[0] - 2 :]
    head[...] = dlt[:2]
    crossing[...] = jnp.where(odd == 0, dlt, act)


def outputs_body(ext, outer, inner, w_two, w_one, clip, cotangent, block_out, grad_clip, strip, shifted, columns):
    odd = lax.axis_index("rows") % 2
    place_rows(strip, ext[0], outer[0], inner[0], odd)
    block_out[...] = clip[...] + convolve(strip, w_two, shifted, columns).reshape(clip.shape)
    place_rows(strip, ext[1], outer[1], inner[1], odd)
    grad_clip[...] = cotangent[...] + convolve(strip, w_one, shifted, columns).reshape(clip.shape)


def grads_body(sending, own, partner, outer, far, active, delta, arrived, first, second, field, wide, turned):
    odd = lax.axis_index("rows") % 2
    y_bit = (lax.axis_index("rows") // 2) % 2
    x_bit = lax.axis_index("tm") % 2
    tall, rows, span, ch = own.shape[1:]
    frames = active.shape[0]
    pick = 1 - odd
    field[:, pl.ds(1 + rows * odd, rows)] = own[pick]
    field[:, pl.ds(1 + rows * (1 - odd), rows)] = partner[pick]
    field[:, odd * (2 * rows + 1)] = outer[pick]
    field[:, (1 - odd) * (2 * rows + 1)] = far[pick]
    flat = field[...].reshape(tall * (2 * rows + 2) * span, ch)
    for c in range(3):
        high, low = halves(moved_column(flat, c - 1, span))
        wide[c, :, :, :, 0:ch] = high.reshape(field.shape)
        wide[c, :, :, :, ch : 2 * ch] = low.reshape(field.shape)
    mine = jnp.where(odd == 0, active[...], delta[...])
    other = arrived[...]
    swap = odd == 1
    upper = jnp.where(swap, other, mine)
    lower = jnp.where(swap, mine, other)
    cells = frames * 2 * rows * span
    joined = jnp.concatenate([upper, lower], 1).reshape(cells, ch).T
    high, low = halves(joined)
    turned[0:ch] = high
    turned[ch : 2 * ch] = low

    def tap_of(group, j):
        tap = jnp.minimum(group * 7 + j, 26)
        a, b, c = tap // 9, (tap // 3) % 3, tap % 3
        piece = wide[c, pl.ds(a, frames), pl.ds(b, 2 * rows)].reshape(cells, 2 * ch)
        product = jnp.dot(turned[...], piece, preferred_element_type=F32)
        left = product[:, :ch] + product[:, ch:]
        return left[:ch] + left[ch:]

    def step(j, carry):
        first[j] = tap_of(y_bit ^ sending, j)
        second[j] = tap_of(2 + (x_bit ^ sending), j)
        return carry

    lax.fori_loop(0, 7, step, 0, unroll=True)


def grads(sending, own, partner, outer, far, active, delta, arrived, name):
    frames, rows, span, ch = active.shape
    out = shaped(7, ch, ch)
    field = (frames + 2, 2 * rows + 2, span, ch)
    return kernel(
        lambda *refs: grads_body(sending, *refs),
        [out, out],
        (own, partner, outer, far, active, delta, arrived),
        scratch=[
            pltpu.VMEM(field, F32),
            pltpu.VMEM((3, *field[:-1], 2 * ch), BF16),
            pltpu.VMEM((2 * ch, frames * 2 * rows * span), BF16),
        ],
        flops=14 * 2 * (2 * ch) ** 2 * frames * 2 * rows * span,
        name=name,
    )


def halve_body(keep_a, keep_b, got_a, got_b, stay_a, go_a, stay_b, go_b):
    x_bit = lax.axis_index("tm") % 2
    y_bit = (lax.axis_index("rows") // 2) % 2
    half = stay_a.shape[0]
    for keep, got, bit, stay, go in ((keep_a, got_a, x_bit, stay_a, go_a), (keep_b, got_b, y_bit, stay_b, go_b)):
        near = pl.ds(pl.multiple_of(bit * half, 8), half)
        away = pl.ds(pl.multiple_of((1 - bit) * half, 8), half)
        go[...] = keep[away] + got[away]
        stay[...] = keep[near] + got[near]


def quarter_body(keep_a, keep_b, got_a, got_b, *outs):
    z = (lax.axis_index("tm") // 2) % 4
    size = outs[0].shape[1]
    for d in range(4):
        part = pl.ds(pl.multiple_of((z ^ d) * size, 8), size)
        outs[d][0] = keep_a[part] + got_a[part]
        outs[d][1] = keep_b[part] + got_b[part]


def total_body(factor, *refs):
    *parts, out = refs
    value = parts[0][...]
    for part in parts[1:]:
        value = value + part[...]
    out[...] = value * factor


def join_quarters_body(q0, q1, q2, q3, out_a, out_b):
    z = (lax.axis_index("tm") // 2) % 4
    size = q0.shape[1]
    for d, quarter in enumerate((q0, q1, q2, q3)):
        part = pl.ds(pl.multiple_of((z ^ d) * size, 8), size)
        out_a[part] = quarter[0]
        out_b[part] = quarter[1]


def join_halves_body(own_a, got_a, own_b, got_b, out_a, out_b):
    x_bit = lax.axis_index("tm") % 2
    y_bit = (lax.axis_index("rows") // 2) % 2
    half = own_a.shape[0]
    for own, got, bit, out in ((own_a, got_a, x_bit, out_a), (own_b, got_b, y_bit, out_b)):
        out[pl.ds(pl.multiple_of(bit * half, 8), half)] = own[...]
        out[pl.ds(pl.multiple_of((1 - bit) * half, 8), half)] = got[...]


def finish_body(late, *refs):
    mine, other = refs[0:2], refs[2:4]
    one, two, turned, sem = refs[-4:]
    odd = lax.axis_index("rows") % 2
    x_bit = lax.axis_index("tm") % 2
    y_bit = (lax.axis_index("rows") // 2) % 2
    groups = (y_bit ^ late, 2 + (x_bit ^ late))
    spots = [(k, j) for k in range(2) for j in range(7)]

    def plain(k, j, source):
        return pltpu.make_async_copy(source.at[j], two.at[26 - (groups[k] * 7 + j)], sem.at[0, k, j])

    def flipped(k, j):
        return pltpu.make_async_copy(turned.at[k, j], one.at[groups[k] * 7 + j], sem.at[1, k, j])

    for k, j in spots:
        inside = groups[k] * 7 + j < 27

        @pl.when(inside & (odd == 0))
        def _():
            plain(k, j, mine[k]).start()

        @pl.when(inside & (odd == 1))
        def _():
            plain(k, j, other[k]).start()

    for k in range(2):
        for j in range(7):
            turned[k, j] = jnp.where(odd == 0, other[k][j], mine[k][j]).T
    for start in (True, False):
        for k, j in spots:

            @pl.when(groups[k] * 7 + j < 27)
            def _():
                if start:
                    flipped(k, j).start()
                else:
                    plain(k, j, mine[k]).wait()
                    flipped(k, j).wait()


def finish(late, mine, other, grads_so_far, name):
    ch = mine[0].shape[-1]
    grad = shaped(27, ch, ch)
    args = [v.reshape(7, ch, ch) for v in (*mine, *other)] + list(grads_so_far)
    return kernel(
        lambda *refs: finish_body(late, *refs),
        [grad, grad],
        args,
        scratch=[pltpu.VMEM((2, 7, ch, ch), F32), pltpu.SemaphoreType.DMA((2, 2, 7))],
        far_in=(4, 5),
        far_out=(0, 1),
        alias={4: 0, 5: 1} if grads_so_far else None,
        name=name,
    )


def tied(*values):
    return list(lax.optimization_barrier(values))


def swapped(value, axis, bits):
    count = lax.axis_size(axis)
    return lax.ppermute(value, axis, [(i, i ^ bits) for i in range(count)])


def per_device(clip, kernel_one, kernel_two, cotangent):
    frames, rows, span, ch = clip.shape
    tm, strips = lax.axis_size("tm"), lax.axis_size("rows")
    factor = 1.0 / math.sqrt(frames * tm * rows * strips * span)
    later = [(i, i + 1) for i in range(tm - 1)]
    earlier = [(i + 1, i) for i in range(tm - 1)]
    across = [pair for i in range(1, strips - 1, 2) for pair in ((i, i + 1), (i + 1, i))]

    strip = shaped(2, rows, span, ch)
    tail, head = kernel(
        ends_body, [strip, strip], (clip, cotangent), scratch=[pltpu.SemaphoreType.DMA((2,))], far_in=(0, 1), name="ends"
    )
    before = lax.ppermute(tail, "tm", later)
    after = lax.ppermute(head, "tm", earlier)
    one, two = kernel_one.reshape(27, ch, ch), kernel_two.reshape(27, ch, ch)
    one_plain, two_turned, clip_near, cot_near = weights(one, two, (clip, cotangent), "weights_early")
    before, after, one_plain, two_turned = tied(before, after, one_plain, two_turned)
    own, edge, _ = pack(clip_near, cot_near, before, after, "pack_inputs")
    outer = lax.ppermute(edge, "rows", across)
    partner = swapped(own, "rows", 1)
    edge_seen, one_late, two_late = tied(edge, one, two)
    two_plain, one_turned = weights(two_late, one_late, (), "weights_late")
    outer, partner, two_plain, one_turned = tied(outer, partner, two_plain, one_turned)
    far = swapped(outer, "rows", 1)

    cell = shaped(frames, rows, span, ch)
    conv_flops = 3 * 2 * frames * rows * span * 27 * ch * ch
    active, delta, tail, head, crossing = kernel(
        forward_body,
        [cell, cell, strip, strip, cell],
        (own, partner, outer, one_plain, two_turned),
        scratch=conv_scratch(frames, rows, span, ch),
        flops=2 * conv_flops,
        name="forward",
    )
    arrived = swapped(crossing, "rows", 1)

    shared = (own, partner, outer, far, active, delta, arrived)
    give_a, give_b = grads(1, *shared, "grads_give")
    got_a = swapped(give_a, "rows", 2)
    got_b = swapped(give_b, "tm", 1)
    keep_a, keep_b = grads(0, *shared, "grads_keep")

    size = 7 * ch
    half = shaped(size // 2, ch)
    stay_a, go_a, stay_b, go_b = kernel(
        halve_body,
        [half] * 4,
        tuple(v.reshape(size, ch) for v in (keep_a, keep_b, got_a, got_b)),
        name="halve",
    )
    got_a = swapped(go_a, "tm", 1)
    got_b = swapped(go_b, "rows", 2)
    quarter = shaped(2, size // 8, ch)
    parts = list(kernel(quarter_body, [quarter] * 4, (stay_a, stay_b, got_a, got_b), name="quarter"))
    parts[0], tail, head = tied(parts[0], tail, head)
    summed = [parts[0]] + [swapped(parts[d], "tm", 2 * d) for d in range(1, 4)]

    before = lax.ppermute(tail, "tm", later)
    after = lax.ppermute(head, "tm", earlier)
    ext, edge, inside = pack(active, delta, before, after, "pack_middle")
    ext, edge, inside, *summed = tied(ext, edge, inside, *summed)

    wider = [("tm", 1 << k) for k in range(3, tm.bit_length() - 1)]
    wider += [("rows", 1 << k) for k in range(2, strips.bit_length() - 1)]
    for axis, bits in wider:
        (shard,) = kernel(lambda *refs: total_body(1.0, *refs), [quarter], summed, name="total")
        summed = [shard, swapped(shard, axis, bits)]
    (shard,) = kernel(lambda *refs: total_body(factor, *refs), [quarter], summed, name="total")

    shard, edge, inside = tied(shard, edge, inside)
    quarters = [shard] + [swapped(shard, "tm", 2 * d) for d in range(1, 4)]
    outer = lax.ppermute(edge, "rows", across)
    inner = swapped(inside, "rows", 1)
    block_out, grad_clip = kernel(
        outputs_body,
        [cell, cell],
        (ext, outer, inner, two_plain, one_turned, clip, cotangent),
        scratch=conv_scratch(frames, rows, span, ch),
        flops=2 * conv_flops,
        name="outputs",
    )
    block_out, grad_clip, *quarters = tied(block_out, grad_clip, *quarters)
    own_a, own_b = kernel(join_quarters_body, [half] * 2, quarters, name="join_quarters")
    got_a = swapped(own_a, "tm", 1)
    got_b = swapped(own_b, "rows", 2)
    full = shaped(size, ch)
    mine = kernel(join_halves_body, [full] * 2, (own_a, got_a, own_b, got_b), name="join_halves")
    got = [swapped(mine[0], "rows", 2), swapped(mine[1], "tm", 1)]
    other = [swapped(v, "rows", 1) for v in mine]
    half_done = finish(0, mine, other, (), "finish_early")
    got[0], got[1], *half_done = tied(*got, *half_done)
    got_other = [swapped(v, "rows", 1) for v in got]
    grad_one, grad_two = finish(1, got, got_other, half_done, "finish_late")
    shape = kernel_one.shape
    return block_out, grad_clip, grad_one.reshape(shape), grad_two.reshape(shape)


def solution(mesh):
    return jax.shard_map(
        per_device,
        mesh=mesh,
        in_specs=(P("tm", "rows", None, None), P(), P(), P("tm", "rows", None, None)),
        out_specs=(P("tm", "rows", None, None), P("tm", "rows", None, None), P(), P()),
        check_vma=False,
    )
```

```python
import math

import jax
import jax.numpy as jnp
from jax import lax
from jax.experimental import pallas as pl
from jax.experimental.pallas import tpu as pltpu
from jax.sharding import PartitionSpec as P

F32, BF16 = jnp.float32, jnp.bfloat16
VM, HBM = pltpu.VMEM, pltpu.HBM


def shaped(*dims, kind=F32):
    return jax.ShapeDtypeStruct(dims, kind)


def kernel(body, outs, args, scratch=(), flops=0, limit=20, far_in=(), far_out=(), alias=None):
    moved = sum(a.size * a.dtype.itemsize for a in (*args, *outs))
    args = [pltpu.with_memory_space_constraint(a, HBM) if i in far_in else a for i, a in enumerate(args)]
    return pl.pallas_call(
        body,
        out_shape=list(outs),
        in_specs=[pl.BlockSpec(memory_space=HBM if i in far_in else VM) for i in range(len(args))],
        out_specs=[pl.BlockSpec(memory_space=HBM if i in far_out else VM) for i in range(len(outs))],
        scratch_shapes=list(scratch),
        input_output_aliases=alias or {},
        compiler_params=pltpu.CompilerParams(vmem_limit_bytes=limit << 20),
        cost_estimate=pl.CostEstimate(flops=flops, bytes_accessed=moved, transcendentals=0),
    )(*args)


def halves(value):
    high = value.astype(BF16)
    return high, (value - high.astype(F32)).astype(BF16)


def moved_column(value, step, span):
    if step == 0:
        return value
    count = value.shape[0]
    column = lax.broadcasted_iota(jnp.int32, value.shape, 0) % span
    edge = span - 1 if step > 0 else 0
    return jnp.where(column == edge, 0.0, pltpu.roll(value, (-step) % count, 0))


def weights_body(plain, turned, *refs):
    count = (len(refs) - 4) // 2
    extra, (plain_out, turned_out), near = refs[:count], refs[count : count + 2], refs[count + 2 : -2]
    held, sem = refs[-2:]
    taps, ch = plain.shape[0], plain.shape[1]
    block = taps // 3
    copies = []
    for k in range(3):
        part = pl.ds(k * block, block)
        for which, source in enumerate((plain, turned)):
            copies.append(pltpu.make_async_copy(source.at[part], held.at[which, part], sem.at[which, k]))
    side = [pltpu.make_async_copy(a, b, sem.at[2, k]) for k, (a, b) in enumerate(zip(extra, near))]
    for copy in (*copies, *side):
        copy.start()

    def step(tap, carry):
        high, low = halves(held[0, tap])
        plain_out[tap, :, 0:ch] = high
        plain_out[tap, :, ch : 2 * ch] = low
        high, low = halves(held[1, tap].T)
        turned_out[taps - 1 - tap, :, 0:ch] = high
        turned_out[taps - 1 - tap, :, ch : 2 * ch] = low
        return carry

    for k in range(3):
        copies[2 * k].wait()
        copies[2 * k + 1].wait()
        lax.fori_loop(k * block, (k + 1) * block, step, 0, unroll=True)
    for copy in side:
        copy.wait()


def weights(plain, turned, extra):
    taps, ch = plain.shape[0], plain.shape[1]
    out = shaped(taps, ch, 2 * ch, kind=BF16)
    return kernel(
        weights_body,
        [out, out, *(shaped(*v.shape) for v in extra)],
        (plain, turned, *extra),
        scratch=[pltpu.VMEM((2, taps, ch, ch), F32), pltpu.SemaphoreType.DMA((3, 3))],
        far_in=range(2 + len(extra)),
    )


def ends_body(first, second, tail, head, sem):
    frames, depth = first.shape[0], tail.shape[0]
    one = pltpu.make_async_copy(first.at[pl.ds(frames - depth, depth)], tail, sem.at[0])
    two = pltpu.make_async_copy(second.at[pl.ds(0, depth)], head, sem.at[1])
    one.start()
    two.start()
    one.wait()
    two.wait()


def pack_body(first, second, before, after, whole, outer, inner=None):
    frames = first.shape[0]
    depth = whole.shape[1] - frames
    lead = before.shape[0] - depth
    rows = first.shape[1]
    odd = lax.axis_index("rows") % 2
    whole[0, depth:] = first[...]
    whole[0, 0:depth] = before[lead:]
    whole[1, 0:frames] = second[...]
    whole[1, frames:] = after[0:depth]
    outer[...] = whole[:, :, odd * (rows - 1)]
    if inner is not None:
        inner[...] = whole[:, :, (1 - odd) * (rows - 1)]


def pack(first, second, before, after, edges):
    frames, rows, span, ch = first.shape
    edge = shaped(2, frames + 2, span, ch)
    return kernel(pack_body, [shaped(2, frames + 2, rows, span, ch)] + [edge] * edges, (first, second, before, after))


def convolve(strip, weight, shifted, columns):
    tall, wide, span, ch = strip.shape
    frames, rows = tall - 2, wide - 2
    cells = frames * rows * span
    flat = strip[...].reshape(tall * wide * span, ch)
    for c in range(3):
        high, low = halves(moved_column(flat, c - 1, span))
        shifted[0, c] = high.reshape(tall, wide, span, ch)
        shifted[1, c] = low.reshape(tall, wide, span, ch)
    for part in range(2):
        for a in range(3):
            for b in range(3):
                for c in range(3):
                    tap = (a * 3 + b) * 3 + c
                    piece = shifted[part, c, a : a + frames, b : b + rows]
                    columns[part, :, tap * ch : (tap + 1) * ch] = piece.reshape(cells, ch)
    matrix = weight[...].reshape(27 * ch, 2 * ch)
    main = jnp.dot(columns[0], matrix, preferred_element_type=F32)
    rest = jnp.dot(columns[1], matrix[:, :ch], preferred_element_type=F32)
    return main[:, :ch] + main[:, ch:] + rest


def conv_scratch(frames, rows, span, ch):
    return [
        pltpu.VMEM((frames + 2, rows + 2, span, ch), F32),
        pltpu.VMEM((2, 3, frames + 2, rows + 2, span, ch), BF16),
        pltpu.VMEM((2, frames * rows * span, 27 * ch), BF16),
    ]


def place_rows(strip, own, outer, inner, odd):
    rows = own.shape[1]
    strip[:, 1 : rows + 1] = own
    strip[:, odd * (rows + 1)] = outer
    strip[:, (1 - odd) * (rows + 1)] = inner


def forward_body(own, partner, outer, w_one, w_two, active, delta, tail, head, crossing, strip, shifted, columns):
    odd = lax.axis_index("rows") % 2
    rows = own.shape[2]
    near = odd * (rows - 1)
    place_rows(strip, own[0], outer[0], partner[0, :, near], odd)
    pre = convolve(strip, w_one, shifted, columns)
    place_rows(strip, own[1], outer[1], partner[1, :, near], odd)
    slope = convolve(strip, w_two, shifted, columns)
    gate = jax.nn.sigmoid(pre)
    act = (pre * gate).reshape(active.shape)
    dlt = (slope * gate * (1.0 + pre * (1.0 - gate))).reshape(delta.shape)
    active[...] = act
    delta[...] = dlt
    tail[...] = act[active.shape[0] - 2 :]
    head[...] = dlt[:2]
    crossing[...] = jnp.where(odd == 0, dlt, act)


def outputs_body(ext, outer, inner, w_two, w_one, clip, cotangent, block_out, grad_clip, strip, shifted, columns):
    odd = lax.axis_index("rows") % 2
    place_rows(strip, ext[0], outer[0], inner[0], odd)
    block_out[...] = clip[...] + convolve(strip, w_two, shifted, columns).reshape(clip.shape)
    place_rows(strip, ext[1], outer[1], inner[1], odd)
    grad_clip[...] = cotangent[...] + convolve(strip, w_one, shifted, columns).reshape(clip.shape)


def grads_body(sending, own, partner, outer, far, active, delta, arrived, first, second, field, wide, turned):
    odd = lax.axis_index("rows") % 2
    y_bit = (lax.axis_index("rows") // 2) % 2
    x_bit = lax.axis_index("tm") % 2
    tall, rows, span, ch = own.shape[1:]
    frames = active.shape[0]
    pick = 1 - odd
    field[:, pl.ds(1 + rows * odd, rows)] = own[pick]
    field[:, pl.ds(1 + rows * (1 - odd), rows)] = partner[pick]
    field[:, odd * (2 * rows + 1)] = outer[pick]
    field[:, (1 - odd) * (2 * rows + 1)] = far[pick]
    flat = field[...].reshape(tall * (2 * rows + 2) * span, ch)
    for c in range(3):
        high, low = halves(moved_column(flat, c - 1, span))
        wide[c, :, :, :, 0:ch] = high.reshape(field.shape)
        wide[c, :, :, :, ch : 2 * ch] = low.reshape(field.shape)
    mine = jnp.where(odd == 0, active[...], delta[...])
    other = arrived[...]
    swap = odd == 1
    upper = jnp.where(swap, other, mine)
    lower = jnp.where(swap, mine, other)
    cells = frames * 2 * rows * span
    joined = jnp.concatenate([upper, lower], 1).reshape(cells, ch).T
    high, low = halves(joined)
    turned[0:ch] = high
    turned[ch : 2 * ch] = low

    def tap_of(group, j):
        tap = jnp.minimum(group * 7 + j, 26)
        a, b, c = tap // 9, (tap // 3) % 3, tap % 3
        piece = wide[c, pl.ds(a, frames), pl.ds(b, 2 * rows)].reshape(cells, 2 * ch)
        product = jnp.dot(turned[...], piece, preferred_element_type=F32)
        left = product[:, :ch] + product[:, ch:]
        return left[:ch] + left[ch:]

    def step(j, carry):
        first[j] = tap_of(y_bit ^ sending, j)
        second[j] = tap_of(2 + (x_bit ^ sending), j)
        return carry

    lax.fori_loop(0, 7, step, 0, unroll=True)


def grads(sending, own, partner, outer, far, active, delta, arrived):
    frames, rows, span, ch = active.shape
    out = shaped(7, ch, ch)
    field = (frames + 2, 2 * rows + 2, span, ch)
    return kernel(
        lambda *refs: grads_body(sending, *refs),
        [out, out],
        (own, partner, outer, far, active, delta, arrived),
        scratch=[
            pltpu.VMEM(field, F32),
            pltpu.VMEM((3, *field[:-1], 2 * ch), BF16),
            pltpu.VMEM((2 * ch, frames * 2 * rows * span), BF16),
        ],
        flops=14 * 2 * (2 * ch) ** 2 * frames * 2 * rows * span,
    )


def halve_body(keep_a, keep_b, got_a, got_b, stay_a, go_a, stay_b, go_b):
    x_bit = lax.axis_index("tm") % 2
    y_bit = (lax.axis_index("rows") // 2) % 2
    half = stay_a.shape[0]
    for keep, got, bit, stay, go in ((keep_a, got_a, x_bit, stay_a, go_a), (keep_b, got_b, y_bit, stay_b, go_b)):
        near = pl.ds(pl.multiple_of(bit * half, 8), half)
        away = pl.ds(pl.multiple_of((1 - bit) * half, 8), half)
        go[...] = keep[away] + got[away]
        stay[...] = keep[near] + got[near]


def quarter_body(keep_a, keep_b, got_a, got_b, *outs):
    z = (lax.axis_index("tm") // 2) % 4
    size = outs[0].shape[1]
    for d in range(4):
        part = pl.ds(pl.multiple_of((z ^ d) * size, 8), size)
        outs[d][0] = keep_a[part] + got_a[part]
        outs[d][1] = keep_b[part] + got_b[part]


def total_body(factor, *refs):
    *parts, out = refs
    value = parts[0][...]
    for part in parts[1:]:
        value = value + part[...]
    out[...] = value * factor


def join_quarters_body(q0, q1, q2, q3, out_a, out_b):
    z = (lax.axis_index("tm") // 2) % 4
    size = q0.shape[1]
    for d, quarter in enumerate((q0, q1, q2, q3)):
        part = pl.ds(pl.multiple_of((z ^ d) * size, 8), size)
        out_a[part] = quarter[0]
        out_b[part] = quarter[1]


def join_halves_body(own_a, got_a, own_b, got_b, out_a, out_b):
    x_bit = lax.axis_index("tm") % 2
    y_bit = (lax.axis_index("rows") // 2) % 2
    half = own_a.shape[0]
    for own, got, bit, out in ((own_a, got_a, x_bit, out_a), (own_b, got_b, y_bit, out_b)):
        out[pl.ds(pl.multiple_of(bit * half, 8), half)] = own[...]
        out[pl.ds(pl.multiple_of((1 - bit) * half, 8), half)] = got[...]


def finish_body(late, *refs):
    mine, other = refs[0:2], refs[2:4]
    one, two, turned, sem = refs[-4:]
    odd = lax.axis_index("rows") % 2
    x_bit = lax.axis_index("tm") % 2
    y_bit = (lax.axis_index("rows") // 2) % 2
    groups = (y_bit ^ late, 2 + (x_bit ^ late))
    spots = [(k, j) for k in range(2) for j in range(7)]

    def plain(k, j, source):
        return pltpu.make_async_copy(source.at[j], two.at[26 - (groups[k] * 7 + j)], sem.at[0, k, j])

    def flipped(k, j):
        return pltpu.make_async_copy(turned.at[k, j], one.at[groups[k] * 7 + j], sem.at[1, k, j])

    for k, j in spots:
        inside = groups[k] * 7 + j < 27

        @pl.when(inside & (odd == 0))
        def _():
            plain(k, j, mine[k]).start()

        @pl.when(inside & (odd == 1))
        def _():
            plain(k, j, other[k]).start()

    for k in range(2):
        for j in range(7):
            turned[k, j] = jnp.where(odd == 0, other[k][j], mine[k][j]).T
    for start in (True, False):
        for k, j in spots:

            @pl.when(groups[k] * 7 + j < 27)
            def _():
                if start:
                    flipped(k, j).start()
                else:
                    plain(k, j, mine[k]).wait()
                    flipped(k, j).wait()


def finish(late, mine, other, grads_so_far):
    ch = mine[0].shape[-1]
    grad = shaped(27, ch, ch)
    args = [v.reshape(7, ch, ch) for v in (*mine, *other)] + list(grads_so_far)
    return list(kernel(
        lambda *refs: finish_body(late, *refs),
        [grad, grad],
        args,
        scratch=[pltpu.VMEM((2, 7, ch, ch), F32), pltpu.SemaphoreType.DMA((2, 2, 7))],
        far_in=(4, 5),
        far_out=(0, 1),
        alias={4: 0, 5: 1} if grads_so_far else None,
    ))


def tied(*values):
    return list(lax.optimization_barrier(values))


def swapped(value, axis, bits):
    return lax.ppermute(value, axis, [(i, i ^ bits) for i in range(lax.axis_size(axis))])


def per_device(clip, kernel_one, kernel_two, cotangent):
    frames, rows, span, ch = clip.shape
    tm, strips = lax.axis_size("tm"), lax.axis_size("rows")
    factor = 1.0 / math.sqrt(frames * tm * rows * strips * span)
    later = [(i, i + 1) for i in range(tm - 1)]
    earlier = [(i + 1, i) for i in range(tm - 1)]
    across = [pair for i in range(1, strips - 1, 2) for pair in ((i, i + 1), (i + 1, i))]

    strip = shaped(2, rows, span, ch)
    tail, head = kernel(
        ends_body, [strip, strip], (clip, cotangent), scratch=[pltpu.SemaphoreType.DMA((2,))], far_in=(0, 1)
    )
    before = lax.ppermute(tail, "tm", later)
    after = lax.ppermute(head, "tm", earlier)
    one, two = kernel_one.reshape(27, ch, ch), kernel_two.reshape(27, ch, ch)
    one_plain, two_turned, clip_near, cot_near = weights(one, two, (clip, cotangent))
    before, after, one_plain, two_turned = tied(before, after, one_plain, two_turned)
    own, edge = pack(clip_near, cot_near, before, after, 1)
    outer = lax.ppermute(edge, "rows", across)
    partner = swapped(own, "rows", 1)
    far = swapped(outer, "rows", 1)

    cell = shaped(frames, rows, span, ch)
    conv_flops = 3 * 2 * frames * rows * span * 27 * ch * ch
    active, delta, tail, head, crossing = kernel(
        forward_body,
        [cell, cell, strip, strip, cell],
        (own, partner, outer, one_plain, two_turned),
        scratch=conv_scratch(frames, rows, span, ch),
        flops=2 * conv_flops,
    )
    arrived = swapped(crossing, "rows", 1)

    shared = (own, partner, outer, far, active, delta, arrived)
    give_a, give_b = grads(1, *shared)
    got_a = swapped(give_a, "rows", 2)
    got_b = swapped(give_b, "tm", 1)
    keep_a, keep_b = grads(0, *shared)
    keep_a, one, two = tied(keep_a, one, two)
    two_plain, one_turned = weights(two, one, ())
    keep_a, two_plain, one_turned = tied(keep_a, two_plain, one_turned)

    size = 7 * ch
    half = shaped(size // 2, ch)
    stay_a, go_a, stay_b, go_b = kernel(
        halve_body, [half] * 4, tuple(v.reshape(size, ch) for v in (keep_a, keep_b, got_a, got_b))
    )
    got_a = swapped(go_a, "tm", 1)
    got_b = swapped(go_b, "rows", 2)
    quarter = shaped(2, size // 8, ch)
    parts = list(kernel(quarter_body, [quarter] * 4, (stay_a, stay_b, got_a, got_b)))
    summed = [parts[0]] + [swapped(parts[d], "tm", 2 * d) for d in range(1, 4)]

    before = lax.ppermute(tail, "tm", later)
    after = lax.ppermute(head, "tm", earlier)
    ext, edge, inside = pack(active, delta, before, after, 2)

    wider = [("tm", 1 << k) for k in range(3, tm.bit_length() - 1)]
    wider += [("rows", 1 << k) for k in range(2, strips.bit_length() - 1)]
    for axis, bits in wider:
        (shard,) = kernel(lambda *refs: total_body(1.0, *refs), [quarter], summed)
        summed = [shard, swapped(shard, axis, bits)]
    (shard,) = kernel(lambda *refs: total_body(factor, *refs), [quarter], summed)

    quarters = [shard] + [swapped(shard, "tm", 2 * d) for d in range(1, 4)]
    outer = lax.ppermute(edge, "rows", across)
    inner = swapped(inside, "rows", 1)
    own_a, own_b = kernel(join_quarters_body, [half] * 2, quarters)
    got_a = swapped(own_a, "tm", 1)
    got_b = swapped(own_b, "rows", 2)
    full = shaped(size, ch)
    mine = kernel(join_halves_body, [full] * 2, (own_a, got_a, own_b, got_b))
    got = [swapped(mine[0], "rows", 2), swapped(mine[1], "tm", 1)]
    other = [swapped(v, "rows", 1) for v in mine]
    half_done = finish(0, mine, other, ())
    half_done[0], outer, inner = tied(half_done[0], outer, inner)
    block_out, grad_clip = kernel(
        outputs_body,
        [cell, cell],
        (ext, outer, inner, two_plain, one_turned, clip, cotangent),
        scratch=conv_scratch(frames, rows, span, ch),
        flops=2 * conv_flops,
    )
    got[0], got[1], block_out, grad_clip = tied(*got, block_out, grad_clip)
    got_other = [swapped(v, "rows", 1) for v in got]
    grad_one, grad_two = finish(1, got, got_other, half_done)
    shape = kernel_one.shape
    return block_out, grad_clip, grad_one.reshape(shape), grad_two.reshape(shape)


def solution(mesh):
    return jax.shard_map(
        per_device,
        mesh=mesh,
        in_specs=(P("tm", "rows", None, None), P(), P(), P("tm", "rows", None, None)),
        out_specs=(P("tm", "rows", None, None), P("tm", "rows", None, None), P(), P()),
        check_vma=False,
    )
```

```python
import math

import jax
import jax.numpy as jnp
from jax import lax
from jax.experimental import pallas as pl
from jax.experimental.pallas import tpu as pltpu
from jax.sharding import PartitionSpec as P

F32, BF16 = jnp.float32, jnp.bfloat16
VM, HBM = pltpu.VMEM, pltpu.HBM


def shaped(*dims, kind=F32):
    return jax.ShapeDtypeStruct(dims, kind)


def kernel(body, outs, args, scratch=(), flops=0, limit=20, far_in=(), far_out=(), alias=None):
    moved = sum(a.size * a.dtype.itemsize for a in (*args, *outs))
    args = [pltpu.with_memory_space_constraint(a, HBM) if i in far_in else a for i, a in enumerate(args)]
    return pl.pallas_call(
        body,
        out_shape=list(outs),
        in_specs=[pl.BlockSpec(memory_space=HBM if i in far_in else VM) for i in range(len(args))],
        out_specs=[pl.BlockSpec(memory_space=HBM if i in far_out else VM) for i in range(len(outs))],
        scratch_shapes=list(scratch),
        input_output_aliases=alias or {},
        compiler_params=pltpu.CompilerParams(vmem_limit_bytes=limit << 20),
        cost_estimate=pl.CostEstimate(flops=flops, bytes_accessed=moved, transcendentals=0),
    )(*args)


def halves(value):
    high = value.astype(BF16)
    return high, (value - high.astype(F32)).astype(BF16)


def moved_column(value, step, span):
    if step == 0:
        return value
    count = value.shape[0]
    column = lax.broadcasted_iota(jnp.int32, value.shape, 0) % span
    edge = span - 1 if step > 0 else 0
    return jnp.where(column == edge, 0.0, pltpu.roll(value, (-step) % count, 0))


def weights_body(plain, turned, *refs):
    count = (len(refs) - 4) // 2
    extra, (plain_out, turned_out), near = refs[:count], refs[count : count + 2], refs[count + 2 : -2]
    held, sem = refs[-2:]
    taps, ch = plain.shape[0], plain.shape[1]
    block = taps // 3
    copies = []
    for k in range(3):
        part = pl.ds(k * block, block)
        for which, source in enumerate((plain, turned)):
            copies.append(pltpu.make_async_copy(source.at[part], held.at[which, part], sem.at[which, k]))
    side = [pltpu.make_async_copy(a, b, sem.at[2, k]) for k, (a, b) in enumerate(zip(extra, near))]
    for copy in (*copies, *side):
        copy.start()

    def step(tap, carry):
        high, low = halves(held[0, tap])
        plain_out[tap, :, 0:ch] = high
        plain_out[tap, :, ch : 2 * ch] = low
        high, low = halves(held[1, tap].T)
        turned_out[taps - 1 - tap, :, 0:ch] = high
        turned_out[taps - 1 - tap, :, ch : 2 * ch] = low
        return carry

    for k in range(3):
        copies[2 * k].wait()
        copies[2 * k + 1].wait()
        lax.fori_loop(k * block, (k + 1) * block, step, 0, unroll=True)
    for copy in side:
        copy.wait()


def weights(plain, turned, extra):
    taps, ch = plain.shape[0], plain.shape[1]
    out = shaped(taps, ch, 2 * ch, kind=BF16)
    return kernel(
        weights_body,
        [out, out, *(shaped(*v.shape) for v in extra)],
        (plain, turned, *extra),
        scratch=[pltpu.VMEM((2, taps, ch, ch), F32), pltpu.SemaphoreType.DMA((3, 3))],
        far_in=range(2 + len(extra)),
    )


def ends_body(first, second, tail, head, sem):
    frames, depth = first.shape[0], tail.shape[0]
    one = pltpu.make_async_copy(first.at[pl.ds(frames - depth, depth)], tail, sem.at[0])
    two = pltpu.make_async_copy(second.at[pl.ds(0, depth)], head, sem.at[1])
    one.start()
    two.start()
    one.wait()
    two.wait()


def pack_body(first, second, before, after, whole, outer, inner=None):
    frames = first.shape[0]
    depth = whole.shape[1] - frames
    lead = before.shape[0] - depth
    rows = first.shape[1]
    odd = lax.axis_index("rows") % 2
    whole[0, depth:] = first[...]
    whole[0, 0:depth] = before[lead:]
    whole[1, 0:frames] = second[...]
    whole[1, frames:] = after[0:depth]
    outer[...] = whole[:, :, odd * (rows - 1)]
    if inner is not None:
        inner[...] = whole[:, :, (1 - odd) * (rows - 1)]


def pack(first, second, before, after, edges):
    frames, rows, span, ch = first.shape
    edge = shaped(2, frames + 2, span, ch)
    return kernel(pack_body, [shaped(2, frames + 2, rows, span, ch)] + [edge] * edges, (first, second, before, after))


def convolve(strip, weight, shifted, columns):
    tall, wide, span, ch = strip.shape
    frames, rows = tall - 2, wide - 2
    cells = frames * rows * span
    flat = strip[...].reshape(tall * wide * span, ch)
    for c in range(3):
        high, low = halves(moved_column(flat, c - 1, span))
        shifted[0, c] = high.reshape(tall, wide, span, ch)
        shifted[1, c] = low.reshape(tall, wide, span, ch)
    for part in range(2):
        for a in range(3):
            for b in range(3):
                for c in range(3):
                    tap = (a * 3 + b) * 3 + c
                    piece = shifted[part, c, a : a + frames, b : b + rows]
                    columns[part, :, tap * ch : (tap + 1) * ch] = piece.reshape(cells, ch)
    matrix = weight[...].reshape(27 * ch, 2 * ch)
    main = jnp.dot(columns[0], matrix, preferred_element_type=F32)
    rest = jnp.dot(columns[1], matrix[:, :ch], preferred_element_type=F32)
    return main[:, :ch] + main[:, ch:] + rest


def conv_scratch(frames, rows, span, ch):
    return [
        pltpu.VMEM((frames + 2, rows + 2, span, ch), F32),
        pltpu.VMEM((2, 3, frames + 2, rows + 2, span, ch), BF16),
        pltpu.VMEM((2, frames * rows * span, 27 * ch), BF16),
    ]


def place_rows(strip, own, outer, inner, odd):
    rows = own.shape[1]
    strip[:, 1 : rows + 1] = own
    strip[:, odd * (rows + 1)] = outer
    strip[:, (1 - odd) * (rows + 1)] = inner


def forward_body(own, partner, outer, w_one, w_two, active, delta, tail, head, crossing, strip, shifted, columns):
    odd = lax.axis_index("rows") % 2
    rows = own.shape[2]
    near = odd * (rows - 1)
    place_rows(strip, own[0], outer[0], partner[0, :, near], odd)
    pre = convolve(strip, w_one, shifted, columns)
    place_rows(strip, own[1], outer[1], partner[1, :, near], odd)
    slope = convolve(strip, w_two, shifted, columns)
    gate = jax.nn.sigmoid(pre)
    act = (pre * gate).reshape(active.shape)
    dlt = (slope * gate * (1.0 + pre * (1.0 - gate))).reshape(delta.shape)
    active[...] = act
    delta[...] = dlt
    tail[...] = act[active.shape[0] - 2 :]
    head[...] = dlt[:2]
    crossing[...] = jnp.where(odd == 0, dlt, act)


def outputs_body(ext, outer, inner, w_two, w_one, clip, cotangent, block_out, grad_clip, strip, shifted, columns):
    odd = lax.axis_index("rows") % 2
    place_rows(strip, ext[0], outer[0], inner[0], odd)
    block_out[...] = clip[...] + convolve(strip, w_two, shifted, columns).reshape(clip.shape)
    place_rows(strip, ext[1], outer[1], inner[1], odd)
    grad_clip[...] = cotangent[...] + convolve(strip, w_one, shifted, columns).reshape(clip.shape)


def bits_of():
    row = lax.axis_index("rows")
    return row % 2, (row // 2) % 2, lax.axis_index("tm") % 2


def turn(value, turned):
    ch = value.shape[-1]
    high, low = halves(value.reshape(-1, ch).T)
    turned[0:ch] = high
    turned[ch : 2 * ch] = low


def tap_sum(tap, turned, wide, frames, start, rows):
    tap = jnp.minimum(tap, 26)
    a, b, c = tap // 9, (tap // 3) % 3, tap % 3
    ch = wide.shape[-1] // 2
    piece = wide[c, pl.ds(a, frames), pl.ds(b + start, rows)].reshape(-1, 2 * ch)
    product = jnp.dot(turned[...], piece, preferred_element_type=F32)
    left = product[:, :ch] + product[:, ch:]
    return left[:ch] + left[ch:]


def near_body(own, partner, outer, far, active, delta, wide, first, second, field, turned):
    odd, y_bit, x_bit = bits_of()
    tall, rows, span, ch = own.shape[1:]
    frames = active.shape[0]
    pick = 1 - odd
    field[:, pl.ds(1 + rows * odd, rows)] = own[pick]
    field[:, pl.ds(1 + rows * (1 - odd), rows)] = partner[pick]
    field[:, odd * (2 * rows + 1)] = outer[pick]
    field[:, (1 - odd) * (2 * rows + 1)] = far[pick]
    flat = field[...].reshape(tall * (2 * rows + 2) * span, ch)
    for c in range(3):
        high, low = halves(moved_column(flat, c - 1, span))
        wide[c, :, :, :, 0:ch] = high.reshape(field.shape)
        wide[c, :, :, :, ch : 2 * ch] = low.reshape(field.shape)
    turn(jnp.where(odd == 0, active[...], delta[...]), turned)
    for j in range(7):
        first[j] = tap_sum((1 - y_bit) * 7 + j, turned, wide, frames, rows * odd, rows)
        second[j] = tap_sum((3 - x_bit) * 7 + j, turned, wide, frames, rows * odd, rows)


def give_body(wide, near_a, near_b, arrived, first, second, turned):
    odd, y_bit, x_bit = bits_of()
    frames, rows = arrived.shape[:2]
    turn(arrived[...], turned)
    for j in range(7):
        first[j] = near_a[j] + tap_sum((1 - y_bit) * 7 + j, turned, wide, frames, rows * (1 - odd), rows)
        second[j] = near_b[j] + tap_sum((3 - x_bit) * 7 + j, turned, wide, frames, rows * (1 - odd), rows)


def keep_body(wide, active, delta, arrived, first, second, turned):
    odd, y_bit, x_bit = bits_of()
    frames, rows = arrived.shape[:2]
    mine = jnp.where(odd == 0, active[...], delta[...])
    other = arrived[...]
    upper = jnp.where(odd == 1, other, mine)
    lower = jnp.where(odd == 1, mine, other)
    turn(jnp.concatenate([upper, lower], 1), turned)
    for j in range(7):
        first[j] = tap_sum(y_bit * 7 + j, turned, wide, frames, 0, 2 * rows)
        second[j] = tap_sum((2 + x_bit) * 7 + j, turned, wide, frames, 0, 2 * rows)


def halve_body(keep_a, keep_b, got_a, got_b, stay_a, go_a, stay_b, go_b):
    x_bit = lax.axis_index("tm") % 2
    y_bit = (lax.axis_index("rows") // 2) % 2
    half = stay_a.shape[0]
    for keep, got, bit, stay, go in ((keep_a, got_a, x_bit, stay_a, go_a), (keep_b, got_b, y_bit, stay_b, go_b)):
        near = pl.ds(pl.multiple_of(bit * half, 8), half)
        away = pl.ds(pl.multiple_of((1 - bit) * half, 8), half)
        go[...] = keep[away] + got[away]
        stay[...] = keep[near] + got[near]


def quarter_body(keep_a, keep_b, got_a, got_b, *outs):
    z = (lax.axis_index("tm") // 2) % 4
    size = outs[0].shape[1]
    for d in range(4):
        part = pl.ds(pl.multiple_of((z ^ d) * size, 8), size)
        outs[d][0] = keep_a[part] + got_a[part]
        outs[d][1] = keep_b[part] + got_b[part]


def total_body(factor, *refs):
    *parts, out = refs
    value = parts[0][...]
    for part in parts[1:]:
        value = value + part[...]
    out[...] = value * factor


def join_quarters_body(q0, q1, q2, q3, out_a, out_b):
    z = (lax.axis_index("tm") // 2) % 4
    size = q0.shape[1]
    for d, quarter in enumerate((q0, q1, q2, q3)):
        part = pl.ds(pl.multiple_of((z ^ d) * size, 8), size)
        out_a[part] = quarter[0]
        out_b[part] = quarter[1]


def join_halves_body(own_a, got_a, own_b, got_b, out_a, out_b):
    x_bit = lax.axis_index("tm") % 2
    y_bit = (lax.axis_index("rows") // 2) % 2
    half = own_a.shape[0]
    for own, got, bit, out in ((own_a, got_a, x_bit, out_a), (own_b, got_b, y_bit, out_b)):
        out[pl.ds(pl.multiple_of(bit * half, 8), half)] = own[...]
        out[pl.ds(pl.multiple_of((1 - bit) * half, 8), half)] = got[...]


def finish_body(late, foreign, *refs):
    sources = refs[:2]
    one, two, turned, sem = refs[-4:]
    odd, y_bit, x_bit = bits_of()
    straight = odd == foreign
    groups = (y_bit ^ late, 2 + (x_bit ^ late))
    spots = [(k, j) for k in range(2) for j in range(7)]

    def plain(k, j):
        return pltpu.make_async_copy(sources[k].at[j], two.at[26 - (groups[k] * 7 + j)], sem.at[k, j])

    def flipped(k, j):
        return pltpu.make_async_copy(turned.at[k, j], one.at[groups[k] * 7 + j], sem.at[k, j])

    def each(make, act):
        for k, j in spots:

            @pl.when(groups[k] * 7 + j < 27)
            def _():
                act(make(k, j))

    @pl.when(straight)
    def _():
        each(plain, lambda copy: copy.start())
        each(plain, lambda copy: copy.wait())

    @pl.when(jnp.logical_not(straight))
    def _():
        for k, j in spots:
            turned[k, j] = sources[k][j].T
        each(flipped, lambda copy: copy.start())
        each(flipped, lambda copy: copy.wait())


def finish(late, foreign, sources, grads_so_far):
    ch = sources[0].shape[-1]
    grad = shaped(27, ch, ch)
    args = [v.reshape(7, ch, ch) for v in sources] + list(grads_so_far)
    return kernel(
        lambda *refs: finish_body(late, foreign, *refs),
        [grad, grad],
        args,
        scratch=[pltpu.VMEM((2, 7, ch, ch), F32), pltpu.SemaphoreType.DMA((2, 7))],
        far_in=(2, 3),
        far_out=(0, 1),
        alias={2: 0, 3: 1} if grads_so_far else None,
    )


def tied(*values):
    return list(lax.optimization_barrier(values))


def swapped(value, axis, bits):
    return lax.ppermute(value, axis, [(i, i ^ bits) for i in range(lax.axis_size(axis))])


def per_device(clip, kernel_one, kernel_two, cotangent):
    frames, rows, span, ch = clip.shape
    tm, strips = lax.axis_size("tm"), lax.axis_size("rows")
    factor = 1.0 / math.sqrt(frames * tm * rows * strips * span)
    later = [(i, i + 1) for i in range(tm - 1)]
    earlier = [(i + 1, i) for i in range(tm - 1)]
    across = [pair for i in range(1, strips - 1, 2) for pair in ((i, i + 1), (i + 1, i))]

    strip = shaped(2, rows, span, ch)
    tail, head = kernel(
        ends_body, [strip, strip], (clip, cotangent), scratch=[pltpu.SemaphoreType.DMA((2,))], far_in=(0, 1)
    )
    before = lax.ppermute(tail, "tm", later)
    after = lax.ppermute(head, "tm", earlier)
    one, two = kernel_one.reshape(27, ch, ch), kernel_two.reshape(27, ch, ch)
    one_plain, two_turned, clip_near, cot_near = weights(one, two, (clip, cotangent))
    before, after, one_plain, two_turned = tied(before, after, one_plain, two_turned)
    own, edge = pack(clip_near, cot_near, before, after, 1)
    outer = lax.ppermute(edge, "rows", across)
    partner = swapped(own, "rows", 1)
    far = swapped(outer, "rows", 1)

    cell = shaped(frames, rows, span, ch)
    conv_flops = 3 * 2 * frames * rows * span * 27 * ch * ch
    active, delta, tail, head, crossing = kernel(
        forward_body,
        [cell, cell, strip, strip, cell],
        (own, partner, outer, one_plain, two_turned),
        scratch=conv_scratch(frames, rows, span, ch),
        flops=2 * conv_flops,
    )
    arrived = swapped(crossing, "rows", 1)

    piece = shaped(7, ch, ch)
    tap_flops = 14 * 2 * (2 * ch) ** 2 * frames * rows * span
    far, active = tied(far, active)
    wide, near_a, near_b = kernel(
        near_body,
        [shaped(3, frames + 2, 2 * rows + 2, span, 2 * ch, kind=BF16), piece, piece],
        (own, partner, outer, far, active, delta),
        scratch=[
            pltpu.VMEM((frames + 2, 2 * rows + 2, span, ch), F32),
            pltpu.VMEM((2 * ch, frames * rows * span), BF16),
        ],
        flops=tap_flops,
    )
    give_a, give_b = kernel(
        give_body,
        [piece, piece],
        (wide, near_a, near_b, arrived),
        scratch=[pltpu.VMEM((2 * ch, frames * rows * span), BF16)],
        flops=tap_flops,
    )
    got_a = swapped(give_a, "rows", 2)
    got_b = swapped(give_b, "tm", 1)
    keep_a, keep_b = kernel(
        keep_body,
        [piece, piece],
        (wide, active, delta, arrived),
        scratch=[pltpu.VMEM((2 * ch, 2 * frames * rows * span), BF16)],
        flops=2 * tap_flops,
    )
    keep_a, one, two = tied(keep_a, one, two)
    two_plain, one_turned = weights(two, one, ())
    keep_a, two_plain, one_turned = tied(keep_a, two_plain, one_turned)

    size = 7 * ch
    half = shaped(size // 2, ch)
    stay_a, go_a, stay_b, go_b = kernel(
        halve_body, [half] * 4, tuple(v.reshape(size, ch) for v in (keep_a, keep_b, got_a, got_b))
    )
    got_a = swapped(go_a, "tm", 1)
    got_b = swapped(go_b, "rows", 2)
    quarter = shaped(2, size // 8, ch)
    parts = list(kernel(quarter_body, [quarter] * 4, (stay_a, stay_b, got_a, got_b)))
    summed = [parts[0]] + [swapped(parts[d], "tm", 2 * d) for d in range(1, 4)]

    before = lax.ppermute(tail, "tm", later)
    after = lax.ppermute(head, "tm", earlier)
    ext, edge, inside = pack(active, delta, before, after, 2)

    wider = [("tm", 1 << k) for k in range(3, tm.bit_length() - 1)]
    wider += [("rows", 1 << k) for k in range(2, strips.bit_length() - 1)]
    for axis, bits in wider:
        (shard,) = kernel(lambda *refs: total_body(1.0, *refs), [quarter], summed)
        summed = [shard, swapped(shard, axis, bits)]
    (shard,) = kernel(lambda *refs: total_body(factor, *refs), [quarter], summed)

    quarters = [shard] + [swapped(shard, "tm", 2 * d) for d in range(1, 4)]
    outer = lax.ppermute(edge, "rows", across)
    inner = swapped(inside, "rows", 1)
    own_a, own_b = kernel(join_quarters_body, [half] * 2, quarters)
    got_a = swapped(own_a, "tm", 1)
    got_b = swapped(own_b, "rows", 2)
    full = shaped(size, ch)
    mine = kernel(join_halves_body, [full] * 2, (own_a, got_a, own_b, got_b))
    got = [swapped(mine[0], "rows", 2), swapped(mine[1], "tm", 1)]
    other = [swapped(v, "rows", 1) for v in mine]
    half_done = finish(0, 0, mine, ())
    half_done = list(finish(0, 1, other, half_done))
    half_done[0], outer, inner = tied(half_done[0], outer, inner)
    block_out, grad_clip = kernel(
        outputs_body,
        [cell, cell],
        (ext, outer, inner, two_plain, one_turned, clip, cotangent),
        scratch=conv_scratch(frames, rows, span, ch),
        flops=2 * conv_flops,
    )
    got[0], got[1], block_out, grad_clip = tied(*got, block_out, grad_clip)
    got_other = [swapped(v, "rows", 1) for v in got]
    half_done = finish(1, 0, got, half_done)
    grad_one, grad_two = finish(1, 1, got_other, half_done)
    shape = kernel_one.shape
    return block_out, grad_clip, grad_one.reshape(shape), grad_two.reshape(shape)


def solution(mesh):
    return jax.shard_map(
        per_device,
        mesh=mesh,
        in_specs=(P("tm", "rows", None, None), P(), P(), P("tm", "rows", None, None)),
        out_specs=(P("tm", "rows", None, None), P("tm", "rows", None, None), P(), P()),
        check_vma=False,
    )
```

```python
import math

import jax
import jax.numpy as jnp
from jax import lax
from jax.experimental import pallas as pl
from jax.experimental.pallas import tpu as pltpu
from jax.sharding import PartitionSpec as P

F32, BF16 = jnp.float32, jnp.bfloat16
VM, HBM = pltpu.VMEM, pltpu.HBM


def shaped(*dims, kind=F32):
    return jax.ShapeDtypeStruct(dims, kind)


def kernel(body, outs, args, scratch=(), flops=0, limit=20, far_in=(), far_out=(), alias=None):
    moved = sum(a.size * a.dtype.itemsize for a in (*args, *outs))
    args = [pltpu.with_memory_space_constraint(a, HBM) if i in far_in else a for i, a in enumerate(args)]
    return pl.pallas_call(
        body,
        out_shape=list(outs),
        in_specs=[pl.BlockSpec(memory_space=HBM if i in far_in else VM) for i in range(len(args))],
        out_specs=[pl.BlockSpec(memory_space=HBM if i in far_out else VM) for i in range(len(outs))],
        scratch_shapes=list(scratch),
        input_output_aliases=alias or {},
        compiler_params=pltpu.CompilerParams(vmem_limit_bytes=limit << 20),
        cost_estimate=pl.CostEstimate(flops=flops, bytes_accessed=moved, transcendentals=0),
    )(*args)


def halves(value):
    high = value.astype(BF16)
    return high, (value - high.astype(F32)).astype(BF16)


def moved_column(value, step, span):
    if step == 0:
        return value
    count = value.shape[0]
    column = lax.broadcasted_iota(jnp.int32, value.shape, 0) % span
    edge = span - 1 if step > 0 else 0
    return jnp.where(column == edge, 0.0, pltpu.roll(value, (-step) % count, 0))


def weights_body(plain, turned, *refs):
    count = max(0, len(refs) - 5)
    extra, (plain_out, turned_out), near = refs[:count], refs[count : count + 2], refs[count + 2 : -2]
    held, sem = refs[-2:]
    taps, ch = plain.shape[0], plain.shape[1]
    block = taps // 3
    copies = []
    for k in range(3):
        part = pl.ds(k * block, block)
        for which, source in enumerate((plain, turned)):
            copies.append(pltpu.make_async_copy(source.at[part], held.at[which, part], sem.at[which, k]))
    side = [pltpu.make_async_copy(a, near[0].at[k], sem.at[2, k]) for k, a in enumerate(extra)]
    for copy in (*copies, *side):
        copy.start()

    def step(tap, carry):
        high, low = halves(held[0, tap])
        plain_out[tap, :, 0:ch] = high
        plain_out[tap, :, ch : 2 * ch] = low
        high, low = halves(held[1, tap].T)
        turned_out[taps - 1 - tap, :, 0:ch] = high
        turned_out[taps - 1 - tap, :, ch : 2 * ch] = low
        return carry

    for k in range(3):
        copies[2 * k].wait()
        copies[2 * k + 1].wait()
        lax.fori_loop(k * block, (k + 1) * block, step, 0, unroll=True)
    for copy in side:
        copy.wait()


def weights(plain, turned, extra):
    taps, ch = plain.shape[0], plain.shape[1]
    out = shaped(taps, ch, 2 * ch, kind=BF16)
    return kernel(
        weights_body,
        [out, out] + [shaped(len(extra), *v.shape) for v in extra[:1]],
        (plain, turned, *extra),
        scratch=[pltpu.VMEM((2, taps, ch, ch), F32), pltpu.SemaphoreType.DMA((3, 3))],
        far_in=range(2 + len(extra)),
    )


def ends_body(first, second, tail, head, edge, sem):
    frames, depth, rows = first.shape[0], tail.shape[0], first.shape[1]
    row = (lax.axis_index("rows") % 2) * (rows - 1)
    pairs = (
        (first.at[pl.ds(frames - depth, depth)], tail),
        (second.at[pl.ds(0, depth)], head),
        (first.at[:, row], edge.at[0]),
        (second.at[:, row], edge.at[1]),
    )
    copies = [pltpu.make_async_copy(a, b, sem.at[k]) for k, (a, b) in enumerate(pairs)]
    for copy in copies:
        copy.start()
    for copy in copies:
        copy.wait()


def rim_body(before, after, halo, rim):
    odd = lax.axis_index("rows") % 2
    halo[0] = before[...]
    halo[1] = after[...]
    rim[...] = halo[:, :, odd * (before.shape[1] - 1)]


def pack_body(first, second, before, after, whole, outer, inner=None):
    frames = first.shape[0]
    depth = whole.shape[1] - frames
    lead = before.shape[0] - depth
    rows = first.shape[1]
    odd = lax.axis_index("rows") % 2
    whole[0, depth:] = first[...]
    whole[0, 0:depth] = before[lead:]
    whole[1, 0:frames] = second[...]
    whole[1, frames:] = after[0:depth]
    outer[...] = whole[:, :, odd * (rows - 1)]
    if inner is not None:
        inner[...] = whole[:, :, (1 - odd) * (rows - 1)]


def pack(first, second, before, after, edges):
    frames, rows, span, ch = first.shape
    edge = shaped(2, frames + 2, span, ch)
    return kernel(pack_body, [shaped(2, frames + 2, rows, span, ch)] + [edge] * edges, (first, second, before, after))


def convolve(strip, weight, shifted, columns, first=0, depth=3):
    tall, wide, span, ch = strip.shape
    frames, rows = tall - depth + 1, wide - 2
    cells = frames * rows * span
    flat = strip[...].reshape(tall * wide * span, ch)
    for c in range(3):
        high, low = halves(moved_column(flat, c - 1, span))
        shifted[0, c] = high.reshape(tall, wide, span, ch)
        shifted[1, c] = low.reshape(tall, wide, span, ch)
    for part in range(2):
        for a in range(depth):
            for b in range(3):
                for c in range(3):
                    tap = (a * 3 + b) * 3 + c
                    piece = shifted[part, c, a : a + frames, b : b + rows]
                    columns[part, :, tap * ch : (tap + 1) * ch] = piece.reshape(cells, ch)
    matrix = weight[9 * first : 9 * (first + depth)].reshape(9 * depth * ch, 2 * ch)
    main = jnp.dot(columns[0], matrix, preferred_element_type=F32)
    rest = jnp.dot(columns[1], matrix[:, :ch], preferred_element_type=F32)
    return main[:, :ch] + main[:, ch:] + rest


def conv_scratch(frames, rows, span, ch, depth=3):
    tall = frames + depth - 1
    return [
        pltpu.VMEM((tall, rows + 2, span, ch), F32),
        pltpu.VMEM((2, 3, tall, rows + 2, span, ch), BF16),
        pltpu.VMEM((2, frames * rows * span, 9 * depth * ch), BF16),
    ]


def place_rows(strip, own, outer, inner, odd):
    rows = own.shape[1]
    strip[:, 1 : rows + 1] = own
    strip[:, odd * (rows + 1)] = outer
    strip[:, (1 - odd) * (rows + 1)] = inner


def own_frames_body(own, outer, partner, w_one, w_two, pre, slope, *scratch):
    odd = lax.axis_index("rows") % 2
    frames, rows = own.shape[1:3]
    inner = odd * (rows - 1)
    for which, (weight, out) in enumerate(((w_one, pre), (w_two, slope))):
        strip, shifted, columns = scratch[3 * which : 3 * which + 3]
        lead = 2 - 2 * which
        place_rows(strip.at[lead : lead + frames], own[which], outer[which], partner[which, :, inner], odd)
        blank = frames * which
        strip[blank : blank + 2] = jnp.zeros((2, *strip.shape[1:]), F32)
        out[...] = convolve(strip, weight, shifted, columns)


def forward_body(pre_own, slope_own, halo, outer, partner, w_one, w_two, active, delta, tail, head, crossing, *scratch):
    odd = lax.axis_index("rows") % 2
    rows = halo.shape[2]
    inner = odd * (rows - 1)
    added = []
    for which, weight in enumerate((w_one, w_two)):
        strip, shifted, columns = scratch[3 * which : 3 * which + 3]
        place_rows(strip.at[which : which + 2], halo[which], outer[which], partner[which, :, inner], odd)
        strip[2 - 2 * which] = jnp.zeros(strip.shape[1:], F32)
        added.append(convolve(strip, weight, shifted, columns, which, 2))
    count = added[0].shape[0]
    rest = pre_own.shape[0] - count
    pre = jnp.concatenate([pre_own[:count] + added[0], pre_own[count:]], 0)
    slope = jnp.concatenate([slope_own[:rest], slope_own[rest:] + added[1]], 0)
    gate = jax.nn.sigmoid(pre)
    act = (pre * gate).reshape(active.shape)
    dlt = (slope * gate * (1.0 + pre * (1.0 - gate))).reshape(delta.shape)
    active[...] = act
    delta[...] = dlt
    tail[...] = act[active.shape[0] - 2 :]
    head[...] = dlt[:2]
    crossing[...] = jnp.where(odd == 0, dlt, act)


def outputs_body(ext, outer, inner, w_two, w_one, clip, cotangent, block_out, grad_clip, strip, shifted, columns):
    odd = lax.axis_index("rows") % 2
    place_rows(strip, ext[0], outer[0], inner[0], odd)
    block_out[...] = clip[...] + convolve(strip, w_two, shifted, columns).reshape(clip.shape)
    place_rows(strip, ext[1], outer[1], inner[1], odd)
    grad_clip[...] = cotangent[...] + convolve(strip, w_one, shifted, columns).reshape(clip.shape)


def bits_of():
    row = lax.axis_index("rows")
    return row % 2, (row // 2) % 2, lax.axis_index("tm") % 2


def turn(value, turned):
    ch = value.shape[-1]
    high, low = halves(value.reshape(-1, ch).T)
    turned[0:ch] = high
    turned[ch : 2 * ch] = low


def tap_sum(tap, turned, wide, frames, start, rows):
    a, b, c = tap // 9, (tap // 3) % 3, tap % 3
    ch = wide.shape[-1] // 2
    piece = wide[c, pl.ds(a, frames), pl.ds(b + start, rows)].reshape(-1, 2 * ch)
    product = jnp.dot(turned[...], piece, preferred_element_type=F32)
    left = product[:, :ch] + product[:, ch:]
    return left[:ch] + left[ch:]


def two_groups(first, second, side_a, side_b, block, sum_of, near=None):
    ch = block.shape[1]
    for j in range(7):
        rows = pl.ds(j * ch, ch)
        value = sum_of(side_a * 7 + j)
        first[rows] = value if near is None else near[0][rows] + value
        block[rows] = sum_of(14 + 6 * side_b + j)
    part = block[pl.ds(pl.multiple_of(side_b * (ch // 2), 8), second.shape[0])]
    second[...] = part if near is None else near[1][...] + part


def near_body(*refs):
    own_parts, (active, delta, wide, first, second, field, turned, block) = refs[:8], refs[8:]
    odd, y_bit, x_bit = bits_of()
    frames, rows, span, ch = active.shape
    tall = frames + 2
    pick = 1 - odd
    for part, (own, partner, outer, far) in enumerate((own_parts[:4], own_parts[4:])):
        span_of = pl.ds(frames * (1 - odd), 2) if part else pl.ds(2 * odd, frames)
        field[span_of, pl.ds(1 + rows * odd, rows)] = own[pick]
        field[span_of, pl.ds(1 + rows * (1 - odd), rows)] = partner[pick]
        field[span_of, odd * (2 * rows + 1)] = outer[pick]
        field[span_of, (1 - odd) * (2 * rows + 1)] = far[pick]
    flat = field[...].reshape(tall * (2 * rows + 2) * span, ch)
    for c in range(3):
        high, low = halves(moved_column(flat, c - 1, span))
        wide[c, :, :, :, 0:ch] = high.reshape(field.shape)
        wide[c, :, :, :, ch : 2 * ch] = low.reshape(field.shape)
    turn(jnp.where(odd == 0, active[...], delta[...]), turned)
    sum_of = lambda tap: tap_sum(tap, turned, wide, frames, rows * odd, rows)
    two_groups(first, second, 1 - y_bit, 1 - x_bit, block, sum_of)


def give_body(wide, near_a, near_b, arrived, first, second, turned, block):
    odd, y_bit, x_bit = bits_of()
    frames, rows = arrived.shape[:2]
    turn(arrived[...], turned)
    sum_of = lambda tap: tap_sum(tap, turned, wide, frames, rows * (1 - odd), rows)
    two_groups(first, second, 1 - y_bit, 1 - x_bit, block, sum_of, (near_a, near_b))


def keep_body(wide, active, delta, arrived, first, second, turned, block):
    odd, y_bit, x_bit = bits_of()
    frames, rows = arrived.shape[:2]
    mine = jnp.where(odd == 0, active[...], delta[...])
    other = arrived[...]
    upper = jnp.where(odd == 1, other, mine)
    lower = jnp.where(odd == 1, mine, other)
    turn(jnp.concatenate([upper, lower], 1), turned)
    sum_of = lambda tap: tap_sum(tap, turned, wide, frames, 0, 2 * rows)
    two_groups(first, second, y_bit, x_bit, block, sum_of)


def halve_body(keep_a, keep_b, got_a, got_b, stay_a, go_a, stay_b, go_b):
    x_bit = lax.axis_index("tm") % 2
    y_bit = (lax.axis_index("rows") // 2) % 2
    for keep, got, bit, stay, go in ((keep_a, got_a, x_bit, stay_a, go_a), (keep_b, got_b, y_bit, stay_b, go_b)):
        half = stay.shape[0]
        near = pl.ds(pl.multiple_of(bit * half, 8), half)
        away = pl.ds(pl.multiple_of((1 - bit) * half, 8), half)
        go[...] = keep[away] + got[away]
        stay[...] = keep[near] + got[near]


def quarter_body(keep_a, keep_b, got_a, got_b, *outs):
    z = (lax.axis_index("tm") // 2) % 4
    for d in range(4):
        start = 0
        for keep, got in ((keep_a, got_a), (keep_b, got_b)):
            size = keep.shape[0] // 4
            part = pl.ds(pl.multiple_of((z ^ d) * size, 8), size)
            outs[d][start : start + size] = keep[part] + got[part]
            start += size


def total_body(factor, *refs):
    *parts, out = refs
    value = parts[0][...]
    for part in parts[1:]:
        value = value + part[...]
    out[...] = value * factor


def join_quarters_body(q0, q1, q2, q3, out_a, out_b):
    z = (lax.axis_index("tm") // 2) % 4
    for d, quarter in enumerate((q0, q1, q2, q3)):
        start = 0
        for out in (out_a, out_b):
            size = out.shape[0] // 4
            out[pl.ds(pl.multiple_of((z ^ d) * size, 8), size)] = quarter[start : start + size]
            start += size


def join_halves_body(own_a, got_a, own_b, got_b, out_a, out_b):
    x_bit = lax.axis_index("tm") % 2
    y_bit = (lax.axis_index("rows") // 2) % 2
    for own, got, bit, out in ((own_a, got_a, x_bit, out_a), (own_b, got_b, y_bit, out_b)):
        half = own.shape[0]
        out[pl.ds(pl.multiple_of(bit * half, 8), half)] = own[...]
        out[pl.ds(pl.multiple_of((1 - bit) * half, 8), half)] = got[...]


def finish_body(late, foreign, *refs):
    first, second = refs[:2]
    one, two, turned, sem = refs[-4:]
    odd, y_bit, x_bit = bits_of()
    straight = odd == foreign
    side_a, side_b = y_bit ^ late, x_bit ^ late
    ch = one.shape[-1]
    half = ch // 2
    spots = [(first, pl.ds(j * ch, ch), side_a * 7 + j) for j in range(7)]
    spots += [(second, pl.ds(pl.multiple_of(side_b * half + j * ch, 8), ch), 14 + 7 * side_b + j) for j in range(6)]

    def shared(side):
        return pl.ds(pl.multiple_of((1 - side) * 6 * ch, 8), half)

    @pl.when(straight)
    def _():
        copies = [pltpu.make_async_copy(v.at[rows], two.at[26 - tap], sem.at[k]) for k, (v, rows, tap) in enumerate(spots)]
        place = pl.ds(pl.multiple_of(side_b * half, 8), half)
        copies.append(pltpu.make_async_copy(second.at[shared(side_b)], two.at[6, place], sem.at[13]))
        for copy in copies:
            copy.start()
        for copy in copies:
            copy.wait()

    @pl.when(jnp.logical_not(straight))
    def _():
        for k, (v, rows, _) in enumerate(spots):
            turned[k] = v[rows].T
        copies = [pltpu.make_async_copy(turned.at[k], one.at[tap], sem.at[k]) for k, (_, _, tap) in enumerate(spots)]
        if late:
            here, there = second[shared(side_b)], refs[2][shared(1 - side_b)]
            upper = jnp.where(side_b == 0, here, there)
            lower = jnp.where(side_b == 0, there, here)
            turned[13] = jnp.concatenate([upper, lower], 0).T
            copies.append(pltpu.make_async_copy(turned.at[13], one.at[20], sem.at[13]))
        for copy in copies:
            copy.start()
        for copy in copies:
            copy.wait()


def finish(late, foreign, sources, grads_so_far):
    ch = sources[0].shape[-1]
    grad = shaped(27, ch, ch)
    count = len(sources)
    return kernel(
        lambda *refs: finish_body(late, foreign, *refs),
        [grad, grad],
        [*sources, *grads_so_far],
        scratch=[pltpu.VMEM((14, ch, ch), F32), pltpu.SemaphoreType.DMA((14,))],
        far_in=(count, count + 1),
        far_out=(0, 1),
        alias={count: 0, count + 1: 1} if grads_so_far else None,
    )


def tied(*values):
    return list(lax.optimization_barrier(values))


def swapped(value, axis, bits):
    return lax.ppermute(value, axis, [(i, i ^ bits) for i in range(lax.axis_size(axis))])


def per_device(clip, kernel_one, kernel_two, cotangent):
    frames, rows, span, ch = clip.shape
    tm, strips = lax.axis_size("tm"), lax.axis_size("rows")
    factor = 1.0 / math.sqrt(frames * tm * rows * strips * span)
    later = [(i, i + 1) for i in range(tm - 1)]
    earlier = [(i + 1, i) for i in range(tm - 1)]
    across = [pair for i in range(1, strips - 1, 2) for pair in ((i, i + 1), (i + 1, i))]

    strip = shaped(2, rows, span, ch)
    cell = shaped(frames, rows, span, ch)
    tail, head, edge = kernel(
        ends_body,
        [strip, strip, shaped(2, frames, span, ch)],
        (clip, cotangent),
        scratch=[pltpu.SemaphoreType.DMA((4,))],
        far_in=(0, 1),
    )
    before = lax.ppermute(tail, "tm", later)
    after = lax.ppermute(head, "tm", earlier)
    outer = lax.ppermute(edge, "rows", across)
    one, two = kernel_one.reshape(27, ch, ch), kernel_two.reshape(27, ch, ch)
    one_plain, two_turned, own = weights(one, two, (clip, cotangent))
    partner = swapped(own, "rows", 1)
    before, after, one_plain, two_turned = tied(before, after, one_plain, two_turned)
    halo, rim = kernel(rim_body, [shaped(2, 2, rows, span, ch), shaped(2, 2, span, ch)], (before, after))
    outer_halo = lax.ppermute(rim, "rows", across)
    partner_halo = swapped(halo, "rows", 1)
    outer, partner, halo = tied(outer, partner, halo)
    far = swapped(outer, "rows", 1)

    conv_flops = 3 * 2 * frames * rows * span * 27 * ch * ch
    flat = shaped(frames * rows * span, ch)
    pre, slope = kernel(
        own_frames_body,
        [flat, flat],
        (own, outer, partner, one_plain, two_turned),
        scratch=conv_scratch(frames, rows, span, ch) * 2,
        flops=2 * conv_flops,
    )
    outer_halo, pre = tied(outer_halo, pre)
    far_halo = swapped(outer_halo, "rows", 1)
    active, delta, tail, head, crossing = kernel(
        forward_body,
        [cell, cell, strip, strip, cell],
        (pre, slope, halo, outer_halo, partner_halo, one_plain, two_turned),
        scratch=conv_scratch(2, rows, span, ch, 2) * 2,
        flops=conv_flops // 2,
    )
    arrived = swapped(crossing, "rows", 1)

    full = [shaped(7 * ch, ch), shaped(6 * ch + ch // 2, ch)]
    half, quarter = ([shaped(v.shape[0] // n, ch) for v in full] for n in (2, 8))
    quarter = shaped(quarter[0].shape[0] + quarter[1].shape[0], ch)
    block = pltpu.VMEM((7 * ch, ch), F32)
    tap_flops = 14 * 2 * (2 * ch) ** 2 * frames * rows * span
    far, active = tied(far, active)
    wide, near_a, near_b = kernel(
        near_body,
        [shaped(3, frames + 2, 2 * rows + 2, span, 2 * ch, kind=BF16), *full],
        (own, partner, outer, far, halo, partner_halo, outer_halo, far_halo, active, delta),
        scratch=[
            pltpu.VMEM((frames + 2, 2 * rows + 2, span, ch), F32),
            pltpu.VMEM((2 * ch, frames * rows * span), BF16),
            block,
        ],
        flops=tap_flops,
    )
    give_a, give_b = kernel(
        give_body,
        full,
        (wide, near_a, near_b, arrived),
        scratch=[pltpu.VMEM((2 * ch, frames * rows * span), BF16), block],
        flops=tap_flops,
    )
    got_a = swapped(give_a, "rows", 2)
    got_b = swapped(give_b, "tm", 1)
    keep_a, keep_b = kernel(
        keep_body,
        full,
        (wide, active, delta, arrived),
        scratch=[pltpu.VMEM((2 * ch, 2 * frames * rows * span), BF16), block],
        flops=2 * tap_flops,
    )
    keep_a, one, two = tied(keep_a, one, two)
    two_plain, one_turned = weights(two, one, ())
    keep_a, two_plain, one_turned = tied(keep_a, two_plain, one_turned)

    stay_a, go_a, stay_b, go_b = kernel(
        halve_body, [half[0], half[0], half[1], half[1]], (keep_a, keep_b, got_a, got_b)
    )
    got_a = swapped(go_a, "tm", 1)
    got_b = swapped(go_b, "rows", 2)
    parts = list(kernel(quarter_body, [quarter] * 4, (stay_a, stay_b, got_a, got_b)))
    summed = [parts[0]] + [swapped(parts[d], "tm", 2 * d) for d in range(1, 4)]

    before = lax.ppermute(tail, "tm", later)
    after = lax.ppermute(head, "tm", earlier)
    ext, edge, inside = pack(active, delta, before, after, 2)

    wider = [("tm", 1 << k) for k in range(3, tm.bit_length() - 1)]
    wider += [("rows", 1 << k) for k in range(2, strips.bit_length() - 1)]
    for axis, bits in wider:
        (shard,) = kernel(lambda *refs: total_body(1.0, *refs), [quarter], summed)
        summed = [shard, swapped(shard, axis, bits)]
    (shard,) = kernel(lambda *refs: total_body(factor, *refs), [quarter], summed)

    quarters = [shard] + [swapped(shard, "tm", 2 * d) for d in range(1, 4)]
    outer = lax.ppermute(edge, "rows", across)
    inner = swapped(inside, "rows", 1)
    own_a, own_b = kernel(join_quarters_body, half, quarters)
    got_a = swapped(own_a, "tm", 1)
    got_b = swapped(own_b, "rows", 2)
    own_a, outer, inner = tied(own_a, outer, inner)
    block_out, grad_clip = kernel(
        outputs_body,
        [cell, cell],
        (ext, outer, inner, two_plain, one_turned, clip, cotangent),
        scratch=conv_scratch(frames, rows, span, ch),
        flops=2 * conv_flops,
    )
    got_a, got_b, block_out, grad_clip = tied(got_a, got_b, block_out, grad_clip)
    mine = kernel(join_halves_body, full, (own_a, got_a, own_b, got_b))
    got = [swapped(mine[0], "rows", 2), swapped(mine[1], "tm", 1)]
    other = [swapped(v, "rows", 1) for v in mine]
    half_done = finish(0, 0, mine, ())
    half_done = list(finish(0, 1, other, half_done))
    got[0], got[1], *half_done = tied(*got, *half_done)
    got_other = [swapped(v, "rows", 1) for v in got]
    half_done = finish(1, 0, [*got, mine[1]], half_done)
    grad_one, grad_two = finish(1, 1, [*got_other, other[1]], half_done)
    shape = kernel_one.shape
    return block_out, grad_clip, grad_one.reshape(shape), grad_two.reshape(shape)


def solution(mesh):
    return jax.shard_map(
        per_device,
        mesh=mesh,
        in_specs=(P("tm", "rows", None, None), P(), P(), P("tm", "rows", None, None)),
        out_specs=(P("tm", "rows", None, None), P("tm", "rows", None, None), P(), P()),
        check_vma=False,
    )
```
